768 devices in a mesh: node: 96 (over z, x, core), local: 8 (over y).
Axes of the slice: x: 4, y: 8, z: 12, core: 2. Of those that a mesh axis runs over, the one named last changes fastest.
Arguments:
- layer_input: bfloat16 [12288, 3584], P('node', 'local'), may hold values from -6 to 6
- output_grad: bfloat16 [12288, 3584], P('node', 'local'), may hold values from -6 to 6
- gate_weight: bfloat16 [96, 3584, 1024], P('node', None, 'local'), may hold values from -0.09375 to 0.09375
- up_weight: bfloat16 [96, 3584, 1024], P('node', None, 'local'), may hold values from -0.09375 to 0.09375
- down_weight: bfloat16 [96, 1024, 3584], P('node', 'local'), may hold values from -0.1875 to 0.1875
- route_offset: int32 [12288, 2], P('node'), may hold values from 0 to 3, all different within a row; in each aligned block of 128 rows (0 to 127, 128 to 255, ...) at most 80 rows name the same one
- gate_fixed: int32 [12288, 2], P('node'), may hold values from 4096 to 65535
Outputs:
- input_grad: bfloat16 [12288, 3584], P('node', 'local')
- gate_grad: float32 [12288, 2], P('node')
The draws below stay inside these ranges and needn't reach their ends.
Inputs may be any that keep to these rules, and one draw needn't show every extreme that they name: `route_offset`: each token names 2 different offsets. Among the 128 tokens of one node no offset is named more than 80 times, and in some node one offset is named exactly 80 times.
All inputs are finite; a program needn't handle non-finite values.
Results may differ from the reference program's by a relative error of at most 0.0049.
Values may be sent and summed in bfloat16 or wider, within the bound.
No kernel may reach another device: no remote copies, remote signals or barrier semaphores. Data moves between devices by JAX's collectives and lax.ppermute only.
A program may use at most 64 MiB of HBM per device.

```python
import math
import jax
import jax.numpy as jnp
import numpy as np
from jax import lax

D = 3584
HID = 1024
GROUP = 4
TOPK = 2
NODE_TOK = 128
CAPACITY = 80
EXPERTS = 96
TOKENS = 12288
N_NODE = 96


def with_ends(entries, own_key, least, high):
    place = [jax.random.randint(jax.random.fold_in(own_key, axis), (), 0, length) for axis, length in enumerate(entries.shape)]
    widest = entries.shape.index(max(entries.shape))
    beside = place[:widest] + [(place[widest] + 1) % entries.shape[widest]] + place[widest + 1:]
    return entries.at[tuple(place)].set(least).at[tuple(beside)].set(high)


def shard_levels(key, shape, shards, low, top_value):
    def one(dim, shards_of):
        draws = jax.random.uniform(jax.random.fold_in(jax.random.fold_in(key, 6), dim), (shards_of,), jnp.float32, low / len(shards), top_value / len(shards))
        return jnp.repeat(jnp.exp(draws), shape[dim] // shards_of).reshape((-1,) + (1,) * (len(shape) - dim - 1))

    gain = one(*shards[0])
    for cut in shards[1:]:
        gain = gain * one(*cut)
    return gain


def routed_block(rng, own, number, rows, count, top, bound, slope):
    sequence = jax.random.permutation(rng, count)
    packed, ordinary = load_shares(count, rows * top, bound, slope, True), load_shares(count, rows * top, bound, slope, False)
    places = jnp.arange(count)

    def named(sizes, turn):
        used = int((sizes > 0).sum())
        fixed = max(1, used // 4)
        moved = fixed + (places - fixed + turn * (used - fixed)) % max(1, count - fixed)
        return jnp.zeros((count,), jnp.int32).at[sequence[jnp.where(places < fixed, places, moved)]].set(jnp.asarray(sizes, jnp.int32))

    sizes = jnp.where(number % 4 == 0, named(packed, number // 4), named(ordinary, number - number // 4 - 1))
    mixed = jax.random.permutation(jax.random.fold_in(own, 3), count)
    donor, taker = mixed[0:count // 2 * 2:2], mixed[1:count // 2 * 2:2]
    margin = jnp.minimum(sizes[donor] - 1, bound - sizes[taker]) // 2
    margin = jnp.where((donor == sequence[0]) | (taker == sequence[0]) | (sizes[taker] == 0), 0, jnp.maximum(margin, 0))
    moved = jax.random.randint(jax.random.fold_in(own, 4), (count // 2,), 0, 1 << 20) % (margin + 1)
    sizes = sizes.at[donor].add(-moved).at[taker].add(moved)
    items = jnp.searchsorted(jnp.cumsum(sizes), jnp.arange(rows * top), side="right").astype(jnp.int32)
    table = items.reshape(top, rows).T
    table = table[jax.random.permutation(jax.random.fold_in(own, 1), rows)]
    turn = jax.random.randint(jax.random.fold_in(own, 2), (rows, 1), 0, top)
    return jnp.take_along_axis(table, (jnp.arange(top)[None, :] + turn) % top, axis=1)


def load_shares(number_of, total, limit, slope, full):
    loads = [(1 << 20) // math.isqrt(standing ** slope) + 1 for standing in range(1, number_of + 1)]
    largest = limit if full else min(limit, max(-(-total // number_of), total * loads[0] // sum(loads)))
    least = 1 if total - largest >= number_of - 1 else 0
    holding, spare = [largest] + [least] * (number_of - 1), total - largest - least * (number_of - 1)
    while spare > 0:
        free = [i for i in range(1, number_of) if holding[i] < largest] or [i for i in range(1, number_of) if holding[i] < limit]
        whole, left = sum([loads[i] for i in free]), spare
        for i in free:
            more = min(limit - holding[i], max(1, left * loads[i] // whole), spare)
            holding[i] = holding[i] + more
            spare = spare - more
    return np.array(holding)


def noise(rng, dims, scale, bound, cuts=(), held_as=jnp.bfloat16):
    values = jax.random.normal(rng, dims, jnp.float32) * scale
    if len(cuts) > 0:
        values = shard_levels(rng, dims, cuts, -0.22, 0.18) * values
    return jnp.clip(values, min=-bound, max=bound).astype(held_as)


def setup_inputs(seed: int = 0) -> dict:
    arg_keys = jax.random.split(jax.random.key(seed), 8)
    layer_input = noise(arg_keys[0], (TOKENS, D), 1.0, 6.0, ((0, 96), (1, 8)))
    output_grad = noise(arg_keys[1], (TOKENS, D), 1.0, 6.0, ((0, 96), (1, 8)))
    gate_weight = noise(arg_keys[2], (EXPERTS, D, HID), D ** -0.5, 0.09375, ((0, 96), (2, 8)))
    up_weight = noise(arg_keys[3], (EXPERTS, D, HID), D ** -0.5, 0.09375, ((0, 96), (2, 8)))
    down_weight = noise(arg_keys[4], (EXPERTS, HID, D), HID ** -0.5, 0.1875, ((0, 96), (1, 8)))
    route_offset_keys = jax.random.split(jax.random.fold_in(arg_keys[5], 1), TOKENS // NODE_TOK)
    route_offset_turns = jax.random.permutation(jax.random.fold_in(arg_keys[5], 3), TOKENS // NODE_TOK)
    route_offset = jax.vmap(lambda own, number: routed_block(jax.random.fold_in(arg_keys[5], 2), own, number, NODE_TOK, GROUP, TOPK, CAPACITY, 2))(route_offset_keys, route_offset_turns).reshape((TOKENS, TOPK))
    gate_fixed = with_ends(jax.random.randint(arg_keys[6], (TOKENS, TOPK), 4096, 65536), jax.random.fold_in(arg_keys[6], 1), 4096, 65535).astype(jnp.int32)
    return dict(layer_input=layer_input, output_grad=output_grad, gate_weight=gate_weight, up_weight=up_weight, down_weight=down_weight, route_offset=route_offset, gate_fixed=gate_fixed)


def packer(chosen, capacity):
    ranks = jnp.cumsum(chosen.astype(jnp.int32)) - 1
    slots = jnp.arange(capacity, dtype=jnp.int32)
    return ((ranks[None, :] == slots[:, None]) & chosen[None, :]).astype(jnp.bfloat16)


def expert_backward(rows_in, rows_grad, gate_cols, up_cols, down_rows):
    gate_pre = jnp.dot(rows_in, gate_cols, preferred_element_type=jnp.float32)
    up_pre = jnp.dot(rows_in, up_cols, preferred_element_type=jnp.float32)
    hidden_grad = lax.dot_general(rows_grad, down_rows, (((1,), (1,)), ((), ())), preferred_element_type=jnp.float32)
    sigmoid = jax.nn.sigmoid(gate_pre)
    swish = gate_pre * sigmoid
    gate_part = jnp.sum(swish * up_pre * hidden_grad, axis=1)
    up_grad = (hidden_grad * swish).astype(jnp.bfloat16)
    pre_grad = (hidden_grad * up_pre * sigmoid * (1.0 + gate_pre * (1.0 - sigmoid))).astype(jnp.bfloat16)
    back = lax.dot_general(pre_grad, gate_cols, (((1,), (1,)), ((), ())), preferred_element_type=jnp.float32)
    back = back + lax.dot_general(up_grad, up_cols, (((1,), (1,)), ((), ())), preferred_element_type=jnp.float32)
    return back, gate_part


def reference(layer_input, output_grad, gate_weight, up_weight, down_weight, route_offset, gate_fixed):
    gates = gate_fixed.astype(jnp.float32) / 65536.0

    def visit(carry, expert):
        input_acc, gate_acc = carry
        gate_cols = lax.dynamic_index_in_dim(gate_weight, expert, 0, keepdims=False)
        up_cols = lax.dynamic_index_in_dim(up_weight, expert, 0, keepdims=False)
        down_rows = lax.dynamic_index_in_dim(down_weight, expert, 0, keepdims=False)
        for offset in range(GROUP):
            source = (expert - offset) % N_NODE
            start = (source * NODE_TOK).astype(jnp.int32)
            rows_in = lax.dynamic_slice_in_dim(layer_input, start, NODE_TOK, 0)
            rows_grad = lax.dynamic_slice_in_dim(output_grad, start, NODE_TOK, 0)
            routes = lax.dynamic_slice_in_dim(route_offset, start, NODE_TOK, 0)
            gate_rows = lax.dynamic_slice_in_dim(gates, start, NODE_TOK, 0)
            hits = routes == offset
            chosen = jnp.any(hits, axis=1)
            weight = jnp.sum(jnp.where(hits, gate_rows, jnp.zeros_like(gate_rows)), axis=1)
            table = packer(chosen, CAPACITY)
            packed_in = jnp.dot(table, rows_in, preferred_element_type=jnp.float32).astype(jnp.bfloat16)
            packed_grad = jnp.dot(table, rows_grad, preferred_element_type=jnp.float32).astype(jnp.bfloat16)
            back, gate_part = expert_backward(packed_in, packed_grad, gate_cols, up_cols, down_rows)
            spread = table.astype(jnp.float32)
            rows_back = lax.dot_general(spread, back, (((0,), (0,)), ((), ())), precision=lax.Precision.HIGHEST)
            gate_back = lax.dot_general(spread, gate_part, (((0,), (0,)), ((), ())), precision=lax.Precision.HIGHEST)
            old_rows = lax.dynamic_slice_in_dim(input_acc, start, NODE_TOK, 0)
            input_acc = lax.dynamic_update_slice_in_dim(input_acc, old_rows + weight[:, None] * rows_back, start, 0)
            old_gate = lax.dynamic_slice_in_dim(gate_acc, start, NODE_TOK, 0)
            added = jnp.where(hits, gate_back[:, None], jnp.zeros_like(old_gate))
            gate_acc = lax.dynamic_update_slice_in_dim(gate_acc, old_gate + added, start, 0)
        return (input_acc, gate_acc), None

    start_acc = (jnp.zeros(layer_input.shape, jnp.float32), jnp.zeros(gate_fixed.shape, jnp.float32))
    final, unused = lax.scan(visit, start_acc, jnp.arange(N_NODE, dtype=jnp.int32))
    return final[0].astype(jnp.bfloat16), final[1]
```

```python
import jax
import jax.numpy as jnp
from jax import lax
from jax.experimental import pallas as pl
from jax.experimental.pallas import tpu as pltpu
from jax.sharding import PartitionSpec as P

GROUP = 4
CAP = 80
TOK = 128
LANE = 128
FEAT = 448
HID = 128
LOCAL = 8
ROUTED = GROUP * CAP
OUT_ROWS = 7 * CAP + 16
PART_ROWS = 3 * ROUTED + 2 * CAP + 16
HOME_ROWS = 4 * CAP + 16
LEVELS = 15
INTERPRET = False

f32 = jnp.float32
bf16 = jnp.bfloat16
NT = (((1,), (1,)), ((), ()))
TN = (((0,), (0,)), ((), ()))


def from_behind(value, axis, steps):
    count = lax.axis_size(axis)
    pairs = [(source, (source + steps) % count) for source in range(count)]
    return lax.ppermute(value, axis, pairs)


def tables(route):
    offsets = lax.broadcasted_iota(jnp.int32, (8, TOK), 0)
    first = jnp.broadcast_to(route[0:1], (8, TOK)) == offsets
    second = jnp.broadcast_to(route[1:2], (8, TOK)) == offsets
    chosen = jnp.where(first | second, 1.0, 0.0)
    before = lax.broadcasted_iota(jnp.int32, (TOK, TOK), 0) < lax.broadcasted_iota(jnp.int32, (TOK, TOK), 1)
    ranks = jnp.dot(chosen.astype(bf16), jnp.where(before, 1.0, 0.0).astype(bf16), preferred_element_type=f32)
    ranks = jnp.where(chosen > 0.5, ranks, -1.0)
    slots = lax.broadcasted_iota(jnp.int32, (CAP, TOK), 0).astype(f32)
    return [
        jnp.where(slots == jnp.broadcast_to(ranks[o : o + 1], (CAP, TOK)), 1.0, 0.0).astype(bf16)
        for o in range(GROUP)
    ]


def level_of(top):
    level = jnp.zeros_like(top)
    for step in range(1, LEVELS):
        level = level + jnp.where(top < 2.0 ** (3 - 8 * step), 1.0, 0.0)
    return level


def power_of(level, sign):
    power = jnp.full_like(level, 2.0 ** (sign * 12))
    for step in range(1, LEVELS):
        power = jnp.where(level > step - 0.5, 2.0 ** (sign * (12 + 8 * step)), power)
    return power


def scaled(values):
    wide = values.astype(f32)
    top = jnp.max(jnp.max(jnp.abs(wide), axis=0, keepdims=True), axis=1, keepdims=True)
    level = level_of(jnp.broadcast_to(top, (1, TOK)))
    return (wide * power_of(level, 1)).astype(bf16), level


def pack_kernel(route_ref, in_ref, grad_ref, *out_refs):
    table = jnp.concatenate(tables(route_ref[...]), axis=0)
    rows_in, level_in = scaled(in_ref[...])
    rows_grad, level_grad = scaled(grad_ref[...])
    tail = jnp.concatenate([rows_in[384:448], rows_grad[384:448]], axis=0)
    parts = [rows_in[0:128], rows_in[128:256], rows_in[256:384]]
    parts += [rows_grad[0:128], rows_grad[128:256], rows_grad[256:384], tail]
    for place, part in enumerate(parts):
        packed = lax.dot_general(table, part, NT, preferred_element_type=f32).astype(bf16)
        for o in range(GROUP):
            out_refs[o][place * CAP : (place + 1) * CAP, :] = packed[o * CAP : (o + 1) * CAP]
    line = lax.broadcasted_iota(jnp.int32, (16, LANE), 0)
    levels = jnp.where(line == 0, level_in, jnp.where(line == 1, level_grad, 0.0)).astype(bf16)
    for o in range(GROUP):
        out_refs[o][7 * CAP : OUT_ROWS, :] = levels


def expert_kernel(got_ref, gate_ref, up_ref, down_ref, out_ref):
    zero_cols = jnp.zeros((64, 2 * HID), bf16)
    zero_half = jnp.zeros((64, HID), bf16)
    pre = jnp.zeros((ROUTED, 2 * HID), f32)
    grad = jnp.zeros((ROUTED, HID), f32)

    def rows_of(d, o, place):
        start = d * GROUP * OUT_ROWS + o * OUT_ROWS + place * CAP
        return got_ref[start : start + CAP, :]

    def column(d, place):
        return jnp.concatenate([rows_of(d, o, place) for o in range(GROUP)], axis=0)

    for d in range(LOCAL):
        low = d * FEAT
        tail = column(d, 6)
        in_a = jnp.concatenate([column(d, 0), column(d, 1)], axis=1)
        in_b = jnp.concatenate([column(d, 2), tail], axis=1)
        grad_a = jnp.concatenate([column(d, 3), column(d, 4)], axis=1)
        grad_b = jnp.concatenate([column(d, 5), tail], axis=1)
        both = jnp.concatenate([gate_ref[low : low + FEAT, :], up_ref[low : low + FEAT, :]], axis=1)
        down = down_ref[low : low + FEAT, :]
        both_b = jnp.concatenate([both[256:448], zero_cols], axis=0)
        down_b = jnp.concatenate([down[256:384], zero_half, down[384:448]], axis=0)
        part = jnp.dot(in_a, both[0:256], preferred_element_type=f32)
        part = part + jnp.dot(in_b, both_b, preferred_element_type=f32)
        part_grad = jnp.dot(grad_a, down[0:256], preferred_element_type=f32)
        part_grad = part_grad + jnp.dot(grad_b, down_b, preferred_element_type=f32)
        back_in = []
        back_grad = []
        for o in range(GROUP):
            start = d * GROUP * OUT_ROWS + o * OUT_ROWS + 7 * CAP
            levels = got_ref[start : start + 16, :].astype(f32)
            inverse_in = power_of(levels[0:1], -1)
            inverse_grad = power_of(levels[1:2], -1)
            back_in.append(part[o * CAP : (o + 1) * CAP] * jnp.concatenate([inverse_in, inverse_in], axis=1))
            back_grad.append(part_grad[o * CAP : (o + 1) * CAP] * inverse_grad)
        pre = pre + jnp.concatenate(back_in, axis=0)
        grad = grad + jnp.concatenate(back_grad, axis=0)
    gate_pre = pre[:, 0:HID]
    up_pre = pre[:, HID : 2 * HID]
    sigmoid = jax.nn.sigmoid(gate_pre)
    swish = gate_pre * sigmoid
    product = swish * up_pre * grad
    up_grad = (grad * swish).astype(bf16)
    pre_grad = (grad * up_pre * sigmoid * (1.0 + gate_pre * (1.0 - sigmoid))).astype(bf16)
    hidden = jnp.concatenate([pre_grad, up_grad], axis=1)
    paired = jnp.concatenate([hidden[0 : 2 * CAP], hidden[2 * CAP : 4 * CAP]], axis=1)
    line = lax.broadcasted_iota(jnp.int32, (16, LANE), 0)
    gate_rows = jnp.zeros((16, LANE), f32)
    for o in range(GROUP):
        piece = jnp.concatenate([product[o * CAP : (o + 1) * CAP], jnp.zeros((LANE - CAP, HID), f32)], axis=0)
        total = lax.dot_general(
            jnp.ones((8, HID), f32), piece, NT, preferred_element_type=f32, precision=lax.Precision.HIGHEST
        )[0:1]
        high = total.astype(bf16).astype(f32)
        gate_rows = jnp.where(line == 2 * o, high, gate_rows)
        gate_rows = jnp.where(line == 2 * o + 1, total - high, gate_rows)
    gate_rows = gate_rows.astype(bf16)
    for d in range(LOCAL):
        low = d * FEAT
        base = d * PART_ROWS
        both = jnp.concatenate([gate_ref[low : low + FEAT, :], up_ref[low : low + FEAT, :]], axis=1)
        wide = lax.dot_general(hidden, both[0:384], NT, preferred_element_type=f32).astype(bf16)
        for j in range(3):
            out_ref[base + j * ROUTED : base + (j + 1) * ROUTED, :] = wide[:, j * LANE : (j + 1) * LANE]
        corner = jnp.concatenate([both[384:448], zero_cols], axis=1)
        other = jnp.concatenate([zero_cols, both[384:448]], axis=1)
        ends = jnp.concatenate([corner, other], axis=0)
        tail = lax.dot_general(paired, ends, NT, preferred_element_type=f32).astype(bf16)
        out_ref[base + 3 * ROUTED : base + 3 * ROUTED + 2 * CAP, :] = tail
        out_ref[base + 3 * ROUTED + 2 * CAP : base + PART_ROWS, :] = gate_rows


def sum_kernel(part_ref, *out_refs):
    def total(start, rows):
        value = part_ref[start : start + rows, :].astype(f32)
        for d in range(1, LOCAL):
            value = value + part_ref[d * PART_ROWS + start : d * PART_ROWS + start + rows, :].astype(f32)
        return value

    for j in range(3):
        for o in range(GROUP):
            out_refs[o][j * CAP : (j + 1) * CAP, :] = total(j * ROUTED + o * CAP, CAP).astype(bf16)
    for half in range(2):
        tail = total(3 * ROUTED + half * CAP, CAP).astype(bf16)
        out_refs[half][3 * CAP : 4 * CAP, :] = tail
        out_refs[half + 2][3 * CAP : 4 * CAP, :] = tail
    gates = total(3 * ROUTED + 2 * CAP, 16)
    line = lax.broadcasted_iota(jnp.int32, (16, LANE), 0)
    for o in range(GROUP):
        gate = gates[2 * o : 2 * o + 1] + gates[2 * o + 1 : 2 * o + 2]
        high = gate.astype(bf16).astype(f32)
        rows = jnp.where(line == 0, high, jnp.where(line == 1, gate - high, 0.0))
        out_refs[o][4 * CAP : HOME_ROWS, :] = rows.astype(bf16)


def unpack_kernel(route_ref, fixed_ref, *refs):
    got_refs = refs[0:GROUP]
    out_ref, gate_ref = refs[GROUP], refs[GROUP + 1]
    route = route_ref[...]
    weights = fixed_ref[...].astype(f32) / 65536.0
    table = tables(route)
    head = jnp.zeros((384, TOK), f32)
    tail = jnp.zeros((64, TOK), f32)
    gate = jnp.zeros((2, TOK), f32)
    for o in range(GROUP):
        got = got_refs[o]
        hits = route == o
        weight = jnp.sum(jnp.where(hits, weights, 0.0), axis=0, keepdims=True)
        rows = jnp.concatenate([got[j * CAP : (j + 1) * CAP, :] for j in range(4)], axis=1)
        back = lax.dot_general(rows, table[o], TN, preferred_element_type=f32)
        head = head + weight * back[0:384]
        tail = tail + weight * (back[384:448] if o < 2 else back[448:512])
        gates = jnp.dot(got[4 * CAP : HOME_ROWS, 0:CAP], table[o], preferred_element_type=f32)
        gate = gate + jnp.where(hits, gates[0:1] + gates[1:2], 0.0)
    out_ref[0:384, :] = head.astype(bf16)
    out_ref[384:448, :] = tail.astype(bf16)
    gate_ref[...] = gate


def call(kernel, outs, *args):
    return pl.pallas_call(kernel, out_shape=outs, interpret=INTERPRET)(*args)


def body(layer_input, output_grad, gate_weight, up_weight, down_weight, route_offset, gate_fixed):
    route = route_offset.T
    packed = call(
        pack_kernel,
        [jax.ShapeDtypeStruct((OUT_ROWS, LANE), bf16)] * GROUP,
        route,
        layer_input.T,
        output_grad.T,
    )
    got = [packed[0]] + [from_behind(packed[o], "node", o) for o in range(1, GROUP)]
    shard = jnp.concatenate(got, axis=0).astype(jnp.float16)
    full = lax.all_gather(shard, "local", axis=0, tiled=True).astype(bf16)
    partial = call(
        expert_kernel,
        jax.ShapeDtypeStruct((LOCAL * PART_ROWS, LANE), bf16),
        full,
        gate_weight[0],
        up_weight[0],
        down_weight[0].T,
    )
    shares = lax.all_to_all(partial, "local", 0, 0, tiled=True)
    summed = call(sum_kernel, [jax.ShapeDtypeStruct((HOME_ROWS, LANE), bf16)] * GROUP, shares)
    home = [summed[0]] + [from_behind(summed[o], "node", -o) for o in range(1, GROUP)]
    input_grad, gate_grad = call(
        unpack_kernel,
        [jax.ShapeDtypeStruct((FEAT, TOK), bf16), jax.ShapeDtypeStruct((2, TOK), f32)],
        route,
        gate_fixed.T,
        *home,
    )
    return input_grad.T, gate_grad.T


def solution(mesh):
    in_specs = (
        P("node", "local"),
        P("node", "local"),
        P("node", None, "local"),
        P("node", None, "local"),
        P("node", "local", None),
        P("node", None),
        P("node", None),
    )
    out_specs = (P("node", "local"), P("node", None))
    return jax.shard_map(body, mesh=mesh, in_specs=in_specs, out_specs=out_specs, check_vma=False)
```

```python
import jax
import jax.numpy as jnp
from jax import lax
from jax.experimental import pallas as pl
from jax.experimental.pallas import tpu as pltpu
from jax.sharding import PartitionSpec as P

GROUP = 4
CAP = 80
TOK = 128
LANE = 128
FEAT = 448
HID = 128
LOCAL = 8
ROUTED = GROUP * CAP
OUT_ROWS = 7 * CAP + 16
PART_ROWS = 3 * ROUTED + 2 * CAP + 16
HOME_ROWS = 4 * CAP + 16
LEVELS = 15
INTERPRET = False

f32 = jnp.float32
bf16 = jnp.bfloat16
NT = (((1,), (1,)), ((), ()))
TN = (((0,), (0,)), ((), ()))


def from_behind(value, axis, steps):
    count = lax.axis_size(axis)
    pairs = [(source, (source + steps) % count) for source in range(count)]
    return lax.ppermute(value, axis, pairs)


def tables(route):
    offsets = lax.broadcasted_iota(jnp.int32, (8, TOK), 0)
    first = jnp.broadcast_to(route[0:1], (8, TOK)) == offsets
    second = jnp.broadcast_to(route[1:2], (8, TOK)) == offsets
    chosen = jnp.where(first | second, 1.0, 0.0)
    before = lax.broadcasted_iota(jnp.int32, (TOK, TOK), 0) < lax.broadcasted_iota(jnp.int32, (TOK, TOK), 1)
    ranks = jnp.dot(chosen.astype(bf16), jnp.where(before, 1.0, 0.0).astype(bf16), preferred_element_type=f32)
    ranks = jnp.where(chosen > 0.5, ranks, -1.0)
    slots = lax.broadcasted_iota(jnp.int32, (CAP, TOK), 0).astype(f32)
    return [
        jnp.where(slots == jnp.broadcast_to(ranks[o : o + 1], (CAP, TOK)), 1.0, 0.0).astype(bf16)
        for o in range(GROUP)
    ]


def level_of(top):
    level = jnp.zeros_like(top)
    for step in range(1, LEVELS):
        level = level + jnp.where(top < 2.0 ** (3 - 8 * step), 1.0, 0.0)
    return level


def power_of(level, sign):
    power = jnp.full_like(level, 2.0 ** (sign * 12))
    for step in range(1, LEVELS):
        power = jnp.where(level > step - 0.5, 2.0 ** (sign * (12 + 8 * step)), power)
    return power


def scaled(values):
    wide = values.astype(f32)
    top = jnp.max(jnp.max(jnp.abs(wide), axis=0, keepdims=True), axis=1, keepdims=True)
    level = level_of(jnp.broadcast_to(top, (1, TOK)))
    return (wide * power_of(level, 1)).astype(bf16), level


def pack_kernel(route_ref, in_ref, grad_ref, *out_refs):
    table = jnp.concatenate(tables(route_ref[...]), axis=0)
    rows_in, level_in = scaled(in_ref[...])
    rows_grad, level_grad = scaled(grad_ref[...])
    tail = jnp.concatenate([rows_in[384:448], rows_grad[384:448]], axis=0)
    parts = [rows_in[0:128], rows_in[128:256], rows_in[256:384]]
    parts += [rows_grad[0:128], rows_grad[128:256], rows_grad[256:384], tail]
    for place, part in enumerate(parts):
        packed = lax.dot_general(table, part, NT, preferred_element_type=f32).astype(bf16)
        for o in range(GROUP):
            out_refs[o][place * CAP : (place + 1) * CAP, :] = packed[o * CAP : (o + 1) * CAP]
    line = lax.broadcasted_iota(jnp.int32, (16, LANE), 0)
    levels = jnp.where(line == 0, level_in, jnp.where(line == 1, level_grad, 0.0)).astype(bf16)
    for o in range(GROUP):
        out_refs[o][7 * CAP : OUT_ROWS, :] = levels


def expert_kernel(got_ref, gate_ref, up_ref, down_ref, out_ref):
    zero_cols = jnp.zeros((64, 2 * HID), bf16)
    zero_half = jnp.zeros((64, HID), bf16)
    pre = jnp.zeros((ROUTED, 2 * HID), f32)
    grad = jnp.zeros((ROUTED, HID), f32)

    def rows_of(d, o, place):
        start = d * GROUP * OUT_ROWS + o * OUT_ROWS + place * CAP
        return got_ref[start : start + CAP, :]

    def column(d, place):
        return jnp.concatenate([rows_of(d, o, place) for o in range(GROUP)], axis=0)

    for d in range(LOCAL):
        low = d * FEAT
        tail = column(d, 6)
        in_a = jnp.concatenate([column(d, 0), column(d, 1)], axis=1)
        in_b = jnp.concatenate([column(d, 2), tail], axis=1)
        grad_a = jnp.concatenate([column(d, 3), column(d, 4)], axis=1)
        grad_b = jnp.concatenate([column(d, 5), tail], axis=1)
        both = jnp.concatenate([gate_ref[low : low + FEAT, :], up_ref[low : low + FEAT, :]], axis=1)
        down = down_ref[low : low + FEAT, :]
        both_b = jnp.concatenate([both[256:448], zero_cols], axis=0)
        down_b = jnp.concatenate([down[256:384], zero_half, down[384:448]], axis=0)
        part = jnp.dot(in_a, both[0:256], preferred_element_type=f32)
        part = part + jnp.dot(in_b, both_b, preferred_element_type=f32)
        part_grad = jnp.dot(grad_a, down[0:256], preferred_element_type=f32)
        part_grad = part_grad + jnp.dot(grad_b, down_b, preferred_element_type=f32)
        back_in = []
        back_grad = []
        for o in range(GROUP):
            start = d * GROUP * OUT_ROWS + o * OUT_ROWS + 7 * CAP
            levels = got_ref[start : start + 16, :].astype(f32)
            inverse_in = power_of(levels[0:1], -1)
            inverse_grad = power_of(levels[1:2], -1)
            back_in.append(part[o * CAP : (o + 1) * CAP] * jnp.concatenate([inverse_in, inverse_in], axis=1))
            back_grad.append(part_grad[o * CAP : (o + 1) * CAP] * inverse_grad)
        pre = pre + jnp.concatenate(back_in, axis=0)
        grad = grad + jnp.concatenate(back_grad, axis=0)
    gate_pre = pre[:, 0:HID]
    up_pre = pre[:, HID : 2 * HID]
    sigmoid = jax.nn.sigmoid(gate_pre)
    swish = gate_pre * sigmoid
    product = swish * up_pre * grad
    up_grad = (grad * swish).astype(bf16)
    pre_grad = (grad * up_pre * sigmoid * (1.0 + gate_pre * (1.0 - sigmoid))).astype(bf16)
    hidden = jnp.concatenate([pre_grad, up_grad], axis=1)
    paired = jnp.concatenate([hidden[0 : 2 * CAP], hidden[2 * CAP : 4 * CAP]], axis=1)
    line = lax.broadcasted_iota(jnp.int32, (16, LANE), 0)
    gate_rows = jnp.zeros((16, LANE), f32)
    for o in range(GROUP):
        piece = jnp.concatenate([product[o * CAP : (o + 1) * CAP], jnp.zeros((LANE - CAP, HID), f32)], axis=0)
        total = lax.dot_general(
            jnp.ones((8, HID), f32), piece, NT, preferred_element_type=f32, precision=lax.Precision.HIGHEST
        )[0:1]
        high = total.astype(bf16).astype(f32)
        gate_rows = jnp.where(line == 2 * o, high, gate_rows)
        gate_rows = jnp.where(line == 2 * o + 1, total - high, gate_rows)
    gate_rows = gate_rows.astype(bf16)
    for d in range(LOCAL):
        low = d * FEAT
        base = d * PART_ROWS
        both = jnp.concatenate([gate_ref[low : low + FEAT, :], up_ref[low : low + FEAT, :]], axis=1)
        wide = lax.dot_general(hidden, both[0:384], NT, preferred_element_type=f32).astype(bf16)
        for j in range(3):
            out_ref[base + j * ROUTED : base + (j + 1) * ROUTED, :] = wide[:, j * LANE : (j + 1) * LANE]
        corner = jnp.concatenate([both[384:448], zero_cols], axis=1)
        other = jnp.concatenate([zero_cols, both[384:448]], axis=1)
        ends = jnp.concatenate([corner, other], axis=0)
        tail = lax.dot_general(paired, ends, NT, preferred_element_type=f32).astype(bf16)
        out_ref[base + 3 * ROUTED : base + 3 * ROUTED + 2 * CAP, :] = tail
        out_ref[base + 3 * ROUTED + 2 * CAP : base + PART_ROWS, :] = gate_rows


def sum_kernel(part_ref, *out_refs):
    def total(start, rows):
        value = part_ref[start : start + rows, :].astype(f32)
        for d in range(1, LOCAL):
            value = value + part_ref[d * PART_ROWS + start : d * PART_ROWS + start + rows, :].astype(f32)
        return value

    for j in range(3):
        for o in range(GROUP):
            out_refs[o][j * CAP : (j + 1) * CAP, :] = total(j * ROUTED + o * CAP, CAP).astype(bf16)
    for half in range(2):
        tail = total(3 * ROUTED + half * CAP, CAP).astype(bf16)
        out_refs[half][3 * CAP : 4 * CAP, :] = tail
        out_refs[half + 2][3 * CAP : 4 * CAP, :] = tail
    gates = total(3 * ROUTED + 2 * CAP, 16)
    line = lax.broadcasted_iota(jnp.int32, (16, LANE), 0)
    for o in range(GROUP):
        gate = gates[2 * o : 2 * o + 1] + gates[2 * o + 1 : 2 * o + 2]
        high = gate.astype(bf16).astype(f32)
        rows = jnp.where(line == 0, high, jnp.where(line == 1, gate - high, 0.0))
        out_refs[o][4 * CAP : HOME_ROWS, :] = rows.astype(bf16)


def unpack_kernel(route_ref, fixed_ref, *refs):
    got_refs = refs[0:GROUP]
    out_ref, gate_ref = refs[GROUP], refs[GROUP + 1]
    route = route_ref[...]
    weights = fixed_ref[...].astype(f32) / 65536.0
    table = tables(route)
    head = jnp.zeros((384, TOK), f32)
    tail = jnp.zeros((64, TOK), f32)
    gate = jnp.zeros((2, TOK), f32)
    for o in range(GROUP):
        got = got_refs[o]
        hits = route == o
        weight = jnp.sum(jnp.where(hits, weights, 0.0), axis=0, keepdims=True)
        rows = jnp.concatenate([got[j * CAP : (j + 1) * CAP, :] for j in range(4)], axis=1)
        back = lax.dot_general(rows, table[o], TN, preferred_element_type=f32)
        head = head + weight * back[0:384]
        tail = tail + weight * (back[384:448] if o < 2 else back[448:512])
        gates = jnp.dot(got[4 * CAP : HOME_ROWS, 0:CAP], table[o], preferred_element_type=f32)
        gate = gate + jnp.where(hits, gates[0:1] + gates[1:2], 0.0)
    out_ref[0:384, :] = head.astype(bf16)
    out_ref[384:448, :] = tail.astype(bf16)
    gate_ref[...] = gate


def call(kernel, outs, *args):
    return pl.pallas_call(kernel, out_shape=outs, interpret=INTERPRET, compiler_params=pltpu.CompilerParams(vmem_limit_bytes=24 * 1024 * 1024))(*args)


def body(layer_input, output_grad, gate_weight, up_weight, down_weight, route_offset, gate_fixed):
    route = route_offset.T
    packed = call(
        pack_kernel,
        [jax.ShapeDtypeStruct((OUT_ROWS, LANE), bf16)] * GROUP,
        route,
        layer_input.T,
        output_grad.T,
    )
    got = [packed[0]] + [from_behind(packed[o], "node", o) for o in range(1, GROUP)]
    shard = jnp.concatenate(got, axis=0).astype(jnp.float16)
    full = lax.all_gather(shard, "local", axis=0, tiled=True).astype(bf16)
    partial = call(
        expert_kernel,
        jax.ShapeDtypeStruct((LOCAL * PART_ROWS, LANE), bf16),
        full,
        gate_weight[0],
        up_weight[0],
        down_weight[0].T,
    )
    shares = lax.all_to_all(partial, "local", 0, 0, tiled=True)
    summed = call(sum_kernel, [jax.ShapeDtypeStruct((HOME_ROWS, LANE), bf16)] * GROUP, shares)
    home = [summed[0]] + [from_behind(summed[o], "node", -o) for o in range(1, GROUP)]
    input_grad, gate_grad = call(
        unpack_kernel,
        [jax.ShapeDtypeStruct((FEAT, TOK), bf16), jax.ShapeDtypeStruct((2, TOK), f32)],
        route,
        gate_fixed.T,
        *home,
    )
    return input_grad.T, gate_grad.T


def solution(mesh):
    in_specs = (
        P("node", "local"),
        P("node", "local"),
        P("node", None, "local"),
        P("node", None, "local"),
        P("node", "local", None),
        P("node", None),
        P("node", None),
    )
    out_specs = (P("node", "local"), P("node", None))
    return jax.shard_map(body, mesh=mesh, in_specs=in_specs, out_specs=out_specs, check_vma=False)
```

```python
import jax
import jax.numpy as jnp
from jax import lax
from jax.experimental import pallas as pl
from jax.experimental.pallas import tpu as pltpu
from jax.sharding import PartitionSpec as P

GROUP = 4
CAP = 80
TOK = 128
LANE = 128
FEAT = 448
HID = 128
LOCAL = 8
ROUTED = GROUP * CAP
OUT_ROWS = 7 * CAP + 16
HIDE_ROWS = 2 * ROUTED + 16
HOME_ROWS = 4 * CAP + 16
LEVELS = 15
TOKEN_CEILING = 3
HIDDEN_CEILING = 24
GATE_CEILING = 44
INTERPRET = False

f32 = jnp.float32
bf16 = jnp.bfloat16
NT = (((1,), (1,)), ((), ()))
TN = (((0,), (0,)), ((), ()))


def from_behind(value, axis, steps):
    count = lax.axis_size(axis)
    pairs = [(source, (source + steps) % count) for source in range(count)]
    return lax.ppermute(value, axis, pairs)


def tables(route):
    offsets = lax.broadcasted_iota(jnp.int32, (8, TOK), 0)
    first = jnp.broadcast_to(route[0:1], (8, TOK)) == offsets
    second = jnp.broadcast_to(route[1:2], (8, TOK)) == offsets
    chosen = jnp.where(first | second, 1.0, 0.0)
    before = lax.broadcasted_iota(jnp.int32, (TOK, TOK), 0) < lax.broadcasted_iota(jnp.int32, (TOK, TOK), 1)
    ranks = jnp.dot(chosen.astype(bf16), jnp.where(before, 1.0, 0.0).astype(bf16), preferred_element_type=f32)
    ranks = jnp.where(chosen > 0.5, ranks, -1.0)
    slots = lax.broadcasted_iota(jnp.int32, (CAP, TOK), 0).astype(f32)
    return [
        jnp.where(slots == jnp.broadcast_to(ranks[o : o + 1], (CAP, TOK)), 1.0, 0.0).astype(bf16)
        for o in range(GROUP)
    ]


def level_of(top, ceiling):
    level = jnp.zeros_like(top)
    for step in range(1, LEVELS):
        level = level + jnp.where(top < 2.0 ** (ceiling - 8 * step), 1.0, 0.0)
    return level


def power_of(level, ceiling, sign):
    base = 15 - ceiling
    power = jnp.full_like(level, 2.0 ** (sign * base))
    for step in range(1, LEVELS):
        power = jnp.where(level > step - 0.5, 2.0 ** (sign * (base + 8 * step)), power)
    return power


def level_for(wide, ceiling):
    top = jnp.max(jnp.max(jnp.abs(wide), axis=0, keepdims=True), axis=1, keepdims=True)
    return level_of(jnp.broadcast_to(top, (1, LANE)), ceiling)


def scaled(values, ceiling):
    wide = values.astype(f32)
    level = level_for(wide, ceiling)
    return (wide * power_of(level, ceiling, 1)).astype(bf16), level


def pack_kernel(route_ref, in_ref, grad_ref, *out_refs):
    table = jnp.concatenate(tables(route_ref[...]), axis=0)
    rows_in, level_in = scaled(in_ref[...], TOKEN_CEILING)
    rows_grad, level_grad = scaled(grad_ref[...], TOKEN_CEILING)
    tail = jnp.concatenate([rows_in[384:448], rows_grad[384:448]], axis=0)
    parts = [rows_in[0:128], rows_in[128:256], rows_in[256:384]]
    parts += [rows_grad[0:128], rows_grad[128:256], rows_grad[256:384], tail]
    for place, part in enumerate(parts):
        packed = lax.dot_general(table, part, NT, preferred_element_type=f32).astype(bf16)
        for o in range(GROUP):
            out_refs[o][place * CAP : (place + 1) * CAP, :] = packed[o * CAP : (o + 1) * CAP]
    line = lax.broadcasted_iota(jnp.int32, (16, LANE), 0)
    levels = jnp.where(line == 0, level_in, jnp.where(line == 1, level_grad, 0.0)).astype(bf16)
    for o in range(GROUP):
        out_refs[o][7 * CAP : OUT_ROWS, :] = levels


def hidden_kernel(got_ref, gate_ref, up_ref, down_ref, out_ref):
    zero_cols = jnp.zeros((64, 2 * HID), bf16)
    zero_half = jnp.zeros((64, HID), bf16)
    pre = jnp.zeros((ROUTED, 2 * HID), f32)
    grad = jnp.zeros((ROUTED, HID), f32)

    def rows_of(d, o, place):
        start = d * GROUP * OUT_ROWS + o * OUT_ROWS + place * CAP
        return got_ref[start : start + CAP, :]

    def column(d, place):
        return jnp.concatenate([rows_of(d, o, place) for o in range(GROUP)], axis=0)

    for d in range(LOCAL):
        low = d * FEAT
        tail = column(d, 6)
        in_a = jnp.concatenate([column(d, 0), column(d, 1)], axis=1)
        in_b = jnp.concatenate([column(d, 2), tail], axis=1)
        grad_a = jnp.concatenate([column(d, 3), column(d, 4)], axis=1)
        grad_b = jnp.concatenate([column(d, 5), tail], axis=1)
        both = jnp.concatenate([gate_ref[low : low + FEAT, :], up_ref[low : low + FEAT, :]], axis=1)
        down = down_ref[low : low + FEAT, :]
        both_b = jnp.concatenate([both[256:448], zero_cols], axis=0)
        down_b = jnp.concatenate([down[256:384], zero_half, down[384:448]], axis=0)
        part = jnp.dot(in_a, both[0:256], preferred_element_type=f32)
        part = part + jnp.dot(in_b, both_b, preferred_element_type=f32)
        part_grad = jnp.dot(grad_a, down[0:256], preferred_element_type=f32)
        part_grad = part_grad + jnp.dot(grad_b, down_b, preferred_element_type=f32)
        back_in = []
        back_grad = []
        for o in range(GROUP):
            start = d * GROUP * OUT_ROWS + o * OUT_ROWS + 7 * CAP
            levels = got_ref[start : start + 16, :].astype(f32)
            inverse_in = power_of(levels[0:1], TOKEN_CEILING, -1)
            inverse_grad = power_of(levels[1:2], TOKEN_CEILING, -1)
            back_in.append(part[o * CAP : (o + 1) * CAP] * jnp.concatenate([inverse_in, inverse_in], axis=1))
            back_grad.append(part_grad[o * CAP : (o + 1) * CAP] * inverse_grad)
        pre = pre + jnp.concatenate(back_in, axis=0)
        grad = grad + jnp.concatenate(back_grad, axis=0)
    gate_pre = pre[:, 0:HID]
    up_pre = pre[:, HID : 2 * HID]
    sigmoid = jax.nn.sigmoid(gate_pre)
    swish = gate_pre * sigmoid
    product = swish * up_pre * grad
    up_grad, level_up = scaled((grad * swish).astype(bf16), HIDDEN_CEILING)
    pre_grad, level_pre = scaled(
        (grad * up_pre * sigmoid * (1.0 + gate_pre * (1.0 - sigmoid))).astype(bf16), HIDDEN_CEILING
    )
    totals = []
    for o in range(GROUP):
        piece = jnp.concatenate([product[o * CAP : (o + 1) * CAP], jnp.zeros((LANE - CAP, HID), f32)], axis=0)
        total = lax.dot_general(
            jnp.ones((8, HID), f32), piece, NT, preferred_element_type=f32, precision=lax.Precision.HIGHEST
        )
        totals.append(total[0:1])
    level_gate = level_for(jnp.concatenate(totals, axis=0), GATE_CEILING)
    power_gate = power_of(level_gate, GATE_CEILING, 1)
    line = lax.broadcasted_iota(jnp.int32, (16, LANE), 0)
    rows = jnp.where(line == 8, level_pre, jnp.where(line == 9, level_up, jnp.where(line == 10, level_gate, 0.0)))
    for o in range(GROUP):
        total = totals[o] * power_gate
        high = total.astype(bf16).astype(f32)
        rows = jnp.where(line == 2 * o, high, jnp.where(line == 2 * o + 1, total - high, rows))
    out_ref[0:ROUTED, :] = pre_grad
    out_ref[ROUTED : 2 * ROUTED, :] = up_grad
    out_ref[2 * ROUTED : HIDE_ROWS, :] = rows.astype(bf16)


def back_kernel(got_ref, gate_ref, up_ref, *out_refs):
    zero_cols = jnp.zeros((64, 2 * HID), bf16)
    head = jnp.zeros((ROUTED, 384), f32)
    tail = jnp.zeros((2 * CAP, LANE), f32)
    gates = jnp.zeros((16, LANE), f32)
    for d in range(LOCAL):
        base = d * HIDE_ROWS
        rows = got_ref[base + 2 * ROUTED : base + HIDE_ROWS, :].astype(f32)
        inverse_pre = power_of(rows[8:9], HIDDEN_CEILING, -1)
        inverse_up = power_of(rows[9:10], HIDDEN_CEILING, -1)
        gates = gates + rows * power_of(rows[10:11], GATE_CEILING, -1)
        pre_grad = (got_ref[base : base + ROUTED, :].astype(f32) * inverse_pre).astype(bf16)
        up_grad = (got_ref[base + ROUTED : base + 2 * ROUTED, :].astype(f32) * inverse_up).astype(bf16)
        hidden = jnp.concatenate([pre_grad, up_grad], axis=1)
        paired = jnp.concatenate([hidden[0 : 2 * CAP], hidden[2 * CAP : 4 * CAP]], axis=1)
        low = d * FEAT
        both = jnp.concatenate([gate_ref[low : low + FEAT, :], up_ref[low : low + FEAT, :]], axis=1)
        head = head + lax.dot_general(hidden, both[0:384], NT, preferred_element_type=f32)
        corner = jnp.concatenate([both[384:448], zero_cols], axis=1)
        other = jnp.concatenate([zero_cols, both[384:448]], axis=1)
        ends = jnp.concatenate([corner, other], axis=0)
        tail = tail + lax.dot_general(paired, ends, NT, preferred_element_type=f32)
    head = head.astype(bf16)
    tail = tail.astype(bf16)
    line = lax.broadcasted_iota(jnp.int32, (16, LANE), 0)
    for o in range(GROUP):
        for j in range(3):
            out_refs[o][j * CAP : (j + 1) * CAP, :] = head[o * CAP : (o + 1) * CAP, j * LANE : (j + 1) * LANE]
        half = o % 2
        out_refs[o][3 * CAP : 4 * CAP, :] = tail[half * CAP : (half + 1) * CAP]
        gate = gates[2 * o : 2 * o + 1] + gates[2 * o + 1 : 2 * o + 2]
        high = gate.astype(bf16).astype(f32)
        rows = jnp.where(line == 0, high, jnp.where(line == 1, gate - high, 0.0))
        out_refs[o][4 * CAP : HOME_ROWS, :] = rows.astype(bf16)


def unpack_kernel(route_ref, fixed_ref, *refs):
    got_refs = refs[0:GROUP]
    out_ref, gate_ref = refs[GROUP], refs[GROUP + 1]
    route = route_ref[...]
    weights = fixed_ref[...].astype(f32) / 65536.0
    table = tables(route)
    head = jnp.zeros((384, TOK), f32)
    tail = jnp.zeros((64, TOK), f32)
    gate = jnp.zeros((2, TOK), f32)
    for o in range(GROUP):
        got = got_refs[o]
        hits = route == o
        weight = jnp.sum(jnp.where(hits, weights, 0.0), axis=0, keepdims=True)
        rows = jnp.concatenate([got[j * CAP : (j + 1) * CAP, :] for j in range(4)], axis=1)
        back = lax.dot_general(rows, table[o], TN, preferred_element_type=f32)
        head = head + weight * back[0:384]
        tail = tail + weight * (back[384:448] if o < 2 else back[448:512])
        gates = jnp.dot(got[4 * CAP : HOME_ROWS, 0:CAP], table[o], preferred_element_type=f32)
        gate = gate + jnp.where(hits, gates[0:1] + gates[1:2], 0.0)
    out_ref[0:384, :] = head.astype(bf16)
    out_ref[384:448, :] = tail.astype(bf16)
    gate_ref[...] = gate


def call(kernel, outs, *args):
    return pl.pallas_call(kernel, out_shape=outs, interpret=INTERPRET, compiler_params=pltpu.CompilerParams(vmem_limit_bytes=24 * 1024 * 1024))(*args)


def body(layer_input, output_grad, gate_weight, up_weight, down_weight, route_offset, gate_fixed):
    route = route_offset.T
    gate_rows = lax.all_to_all(gate_weight[0], "local", 0, 0, tiled=True)
    up_rows = lax.all_to_all(up_weight[0], "local", 0, 0, tiled=True)
    packed = call(
        pack_kernel,
        [jax.ShapeDtypeStruct((OUT_ROWS, LANE), bf16)] * GROUP,
        route,
        layer_input.T,
        output_grad.T,
    )
    got = [packed[0]] + [from_behind(packed[o], "node", o) for o in range(1, GROUP)]
    shard = jnp.concatenate(got, axis=0).astype(jnp.float16)
    full = lax.all_gather(shard, "local", axis=0, tiled=True).astype(bf16)
    hidden = call(
        hidden_kernel,
        jax.ShapeDtypeStruct((HIDE_ROWS, LANE), bf16),
        full,
        gate_weight[0],
        up_weight[0],
        down_weight[0].T,
    )
    spread = lax.all_gather(hidden.astype(jnp.float16), "local", axis=0, tiled=True).astype(bf16)
    summed = call(
        back_kernel, [jax.ShapeDtypeStruct((HOME_ROWS, LANE), bf16)] * GROUP, spread, gate_rows, up_rows
    )
    home = [summed[0]] + [from_behind(summed[o], "node", -o) for o in range(1, GROUP)]
    input_grad, gate_grad = call(
        unpack_kernel,
        [jax.ShapeDtypeStruct((FEAT, TOK), bf16), jax.ShapeDtypeStruct((2, TOK), f32)],
        route,
        gate_fixed.T,
        *home,
    )
    return input_grad.T, gate_grad.T


def solution(mesh):
    in_specs = (
        P("node", "local"),
        P("node", "local"),
        P("node", None, "local"),
        P("node", None, "local"),
        P("node", "local", None),
        P("node", None),
        P("node", None),
    )
    out_specs = (P("node", "local"), P("node", None))
    return jax.shard_map(body, mesh=mesh, in_specs=in_specs, out_specs=out_specs, check_vma=False)
```

```python
import jax
import jax.numpy as jnp
from jax import lax
from jax.experimental import pallas as pl
from jax.experimental.pallas import tpu as pltpu
from jax.sharding import PartitionSpec as P

GROUP = 4
CAP = 80
TOK = 128
LANE = 128
FEAT = 448
HID = 128
LOCAL = 8
ROUTED = GROUP * CAP
OUT_ROWS = 7 * CAP + 16
HIDE_ROWS = 2 * ROUTED + 16
HOME_ROWS = 4 * CAP + 16
PAIR_ROWS = 2 * FEAT
LEVELS = 15
TOKEN_CEILING = 3
HIDDEN_CEILING = 24
GATE_CEILING = 44
INTERPRET = False

f32 = jnp.float32
bf16 = jnp.bfloat16
NT = (((1,), (1,)), ((), ()))
TN = (((0,), (0,)), ((), ()))


def from_behind(value, axis, steps):
    count = lax.axis_size(axis)
    pairs = [(source, (source + steps) % count) for source in range(count)]
    return lax.ppermute(value, axis, pairs)


def tables(route):
    offsets = lax.broadcasted_iota(jnp.int32, (8, TOK), 0)
    first = jnp.broadcast_to(route[0:1], (8, TOK)) == offsets
    second = jnp.broadcast_to(route[1:2], (8, TOK)) == offsets
    chosen = jnp.where(first | second, 1.0, 0.0)
    before = lax.broadcasted_iota(jnp.int32, (TOK, TOK), 0) < lax.broadcasted_iota(jnp.int32, (TOK, TOK), 1)
    ranks = jnp.dot(chosen.astype(bf16), jnp.where(before, 1.0, 0.0).astype(bf16), preferred_element_type=f32)
    ranks = jnp.where(chosen > 0.5, ranks, -1.0)
    slots = lax.broadcasted_iota(jnp.int32, (CAP, TOK), 0).astype(f32)
    return [
        jnp.where(slots == jnp.broadcast_to(ranks[o : o + 1], (CAP, TOK)), 1.0, 0.0).astype(bf16)
        for o in range(GROUP)
    ]


def level_of(top, ceiling):
    level = jnp.zeros_like(top)
    for step in range(1, LEVELS):
        level = level + jnp.where(top < 2.0 ** (ceiling - 8 * step), 1.0, 0.0)
    return level


def power_of(level, ceiling, sign):
    base = 15 - ceiling
    power = jnp.full_like(level, 2.0 ** (sign * base))
    for step in range(1, LEVELS):
        power = jnp.where(level > step - 0.5, 2.0 ** (sign * (base + 8 * step)), power)
    return power


def level_for(wide, ceiling):
    top = jnp.max(jnp.max(jnp.abs(wide), axis=0, keepdims=True), axis=1, keepdims=True)
    return level_of(jnp.broadcast_to(top, (1, LANE)), ceiling)


def scaled(values, ceiling):
    wide = values.astype(f32)
    level = level_for(wide, ceiling)
    return (wide * power_of(level, ceiling, 1)).astype(bf16), level


def pack_kernel(route_ref, in_ref, grad_ref, *out_refs):
    table = jnp.concatenate(tables(route_ref[...]), axis=0)
    rows_in, level_in = scaled(in_ref[...], TOKEN_CEILING)
    rows_grad, level_grad = scaled(grad_ref[...], TOKEN_CEILING)
    tail = jnp.concatenate([rows_in[384:448], rows_grad[384:448]], axis=0)
    parts = [rows_in[0:128], rows_in[128:256], rows_in[256:384]]
    parts += [rows_grad[0:128], rows_grad[128:256], rows_grad[256:384], tail]
    for place, part in enumerate(parts):
        packed = lax.dot_general(table, part, NT, preferred_element_type=f32).astype(bf16)
        for o in range(GROUP):
            out_refs[o][place * CAP : (place + 1) * CAP, :] = packed[o * CAP : (o + 1) * CAP]
    line = lax.broadcasted_iota(jnp.int32, (16, LANE), 0)
    levels = jnp.where(line == 0, level_in, jnp.where(line == 1, level_grad, 0.0)).astype(bf16)
    for o in range(GROUP):
        out_refs[o][7 * CAP : OUT_ROWS, :] = levels


def both_of(pair_ref, d):
    start = d * PAIR_ROWS
    return jnp.concatenate(
        [pair_ref[start : start + FEAT, :], pair_ref[start + FEAT : start + PAIR_ROWS, :]], axis=1
    )


def hidden_kernel(got_ref, pair_ref, down_ref, out_ref):
    zero_cols = jnp.zeros((64, 2 * HID), bf16)
    zero_half = jnp.zeros((64, HID), bf16)
    pre = jnp.zeros((ROUTED, 2 * HID), f32)
    grad = jnp.zeros((ROUTED, HID), f32)

    def rows_of(d, o, place):
        start = d * GROUP * OUT_ROWS + o * OUT_ROWS + place * CAP
        return got_ref[start : start + CAP, :]

    def column(d, place):
        return jnp.concatenate([rows_of(d, o, place) for o in range(GROUP)], axis=0)

    for d in range(LOCAL):
        low = d * FEAT
        tail = column(d, 6)
        in_a = jnp.concatenate([column(d, 0), column(d, 1)], axis=1)
        in_b = jnp.concatenate([column(d, 2), tail], axis=1)
        grad_a = jnp.concatenate([column(d, 3), column(d, 4)], axis=1)
        grad_b = jnp.concatenate([column(d, 5), tail], axis=1)
        both = both_of(pair_ref, d)
        down = down_ref[low : low + FEAT, :]
        both_b = jnp.concatenate([both[256:448], zero_cols], axis=0)
        down_b = jnp.concatenate([down[256:384], zero_half, down[384:448]], axis=0)
        part = jnp.dot(in_a, both[0:256], preferred_element_type=f32)
        part = part + jnp.dot(in_b, both_b, preferred_element_type=f32)
        part_grad = jnp.dot(grad_a, down[0:256], preferred_element_type=f32)
        part_grad = part_grad + jnp.dot(grad_b, down_b, preferred_element_type=f32)
        back_in = []
        back_grad = []
        for o in range(GROUP):
            start = d * GROUP * OUT_ROWS + o * OUT_ROWS + 7 * CAP
            levels = got_ref[start : start + 16, :].astype(f32)
            inverse_in = power_of(levels[0:1], TOKEN_CEILING, -1)
            inverse_grad = power_of(levels[1:2], TOKEN_CEILING, -1)
            back_in.append(part[o * CAP : (o + 1) * CAP] * jnp.concatenate([inverse_in, inverse_in], axis=1))
            back_grad.append(part_grad[o * CAP : (o + 1) * CAP] * inverse_grad)
        pre = pre + jnp.concatenate(back_in, axis=0)
        grad = grad + jnp.concatenate(back_grad, axis=0)
    gate_pre = pre[:, 0:HID]
    up_pre = pre[:, HID : 2 * HID]
    sigmoid = jax.nn.sigmoid(gate_pre)
    swish = gate_pre * sigmoid
    product = swish * up_pre * grad
    up_grad, level_up = scaled((grad * swish).astype(bf16), HIDDEN_CEILING)
    pre_grad, level_pre = scaled(
        (grad * up_pre * sigmoid * (1.0 + gate_pre * (1.0 - sigmoid))).astype(bf16), HIDDEN_CEILING
    )
    totals = []
    for o in range(GROUP):
        piece = jnp.concatenate([product[o * CAP : (o + 1) * CAP], jnp.zeros((LANE - CAP, HID), f32)], axis=0)
        total = lax.dot_general(
            jnp.ones((8, HID), f32), piece, NT, preferred_element_type=f32, precision=lax.Precision.HIGHEST
        )
        totals.append(total[0:1])
    level_gate = level_for(jnp.concatenate(totals, axis=0), GATE_CEILING)
    power_gate = power_of(level_gate, GATE_CEILING, 1)
    line = lax.broadcasted_iota(jnp.int32, (16, LANE), 0)
    rows = jnp.where(line == 8, level_pre, jnp.where(line == 9, level_up, jnp.where(line == 10, level_gate, 0.0)))
    for o in range(GROUP):
        total = totals[o] * power_gate
        high = total.astype(bf16).astype(f32)
        rows = jnp.where(line == 2 * o, high, jnp.where(line == 2 * o + 1, total - high, rows))
    out_ref[0:ROUTED, :] = pre_grad
    out_ref[ROUTED : 2 * ROUTED, :] = up_grad
    out_ref[2 * ROUTED : HIDE_ROWS, :] = rows.astype(bf16)


def back_kernel(got_ref, pair_ref, *out_refs):
    zero_cols = jnp.zeros((64, 2 * HID), bf16)
    head = jnp.zeros((ROUTED, 384), f32)
    tail = jnp.zeros((2 * CAP, LANE), f32)
    gates = jnp.zeros((16, LANE), f32)
    for d in range(LOCAL):
        base = d * HIDE_ROWS
        rows = got_ref[base + 2 * ROUTED : base + HIDE_ROWS, :].astype(f32)
        inverse_pre = power_of(rows[8:9], HIDDEN_CEILING, -1)
        inverse_up = power_of(rows[9:10], HIDDEN_CEILING, -1)
        gates = gates + rows * power_of(rows[10:11], GATE_CEILING, -1)
        pre_grad = (got_ref[base : base + ROUTED, :].astype(f32) * inverse_pre).astype(bf16)
        up_grad = (got_ref[base + ROUTED : base + 2 * ROUTED, :].astype(f32) * inverse_up).astype(bf16)
        hidden = jnp.concatenate([pre_grad, up_grad], axis=1)
        paired = jnp.concatenate([hidden[0 : 2 * CAP], hidden[2 * CAP : 4 * CAP]], axis=1)
        both = both_of(pair_ref, d)
        head = head + lax.dot_general(hidden, both[0:384], NT, preferred_element_type=f32)
        corner = jnp.concatenate([both[384:448], zero_cols], axis=1)
        other = jnp.concatenate([zero_cols, both[384:448]], axis=1)
        ends = jnp.concatenate([corner, other], axis=0)
        tail = tail + lax.dot_general(paired, ends, NT, preferred_element_type=f32)
    head = head.astype(bf16)
    tail = tail.astype(bf16)
    line = lax.broadcasted_iota(jnp.int32, (16, LANE), 0)
    for o in range(GROUP):
        for j in range(3):
            out_refs[o][j * CAP : (j + 1) * CAP, :] = head[o * CAP : (o + 1) * CAP, j * LANE : (j + 1) * LANE]
        half = o % 2
        out_refs[o][3 * CAP : 4 * CAP, :] = tail[half * CAP : (half + 1) * CAP]
        gate = gates[2 * o : 2 * o + 1] + gates[2 * o + 1 : 2 * o + 2]
        high = gate.astype(bf16).astype(f32)
        rows = jnp.where(line == 0, high, jnp.where(line == 1, gate - high, 0.0))
        out_refs[o][4 * CAP : HOME_ROWS, :] = rows.astype(bf16)


def unpack_kernel(route_ref, fixed_ref, *refs):
    got_refs = refs[0:GROUP]
    out_ref, gate_ref = refs[GROUP], refs[GROUP + 1]
    route = route_ref[...]
    weights = fixed_ref[...].astype(f32) / 65536.0
    table = tables(route)
    head = jnp.zeros((384, TOK), f32)
    tail = jnp.zeros((64, TOK), f32)
    gate = jnp.zeros((2, TOK), f32)
    for o in range(GROUP):
        got = got_refs[o]
        hits = route == o
        weight = jnp.sum(jnp.where(hits, weights, 0.0), axis=0, keepdims=True)
        rows = jnp.concatenate([got[j * CAP : (j + 1) * CAP, :] for j in range(4)], axis=1)
        back = lax.dot_general(rows, table[o], TN, preferred_element_type=f32)
        head = head + weight * back[0:384]
        tail = tail + weight * (back[384:448] if o < 2 else back[448:512])
        gates = jnp.dot(got[4 * CAP : HOME_ROWS, 0:CAP], table[o], preferred_element_type=f32)
        gate = gate + jnp.where(hits, gates[0:1] + gates[1:2], 0.0)
    out_ref[0:384, :] = head.astype(bf16)
    out_ref[384:448, :] = tail.astype(bf16)
    gate_ref[...] = gate


def call(kernel, outs, *args):
    return pl.pallas_call(kernel, out_shape=outs, interpret=INTERPRET, compiler_params=pltpu.CompilerParams(vmem_limit_bytes=24 * 1024 * 1024))(*args)


def body(layer_input, output_grad, gate_weight, up_weight, down_weight, route_offset, gate_fixed):
    route = route_offset.T
    pairs = jnp.concatenate(
        [gate_weight[0].reshape(LOCAL, FEAT, HID), up_weight[0].reshape(LOCAL, FEAT, HID)], axis=1
    ).reshape(LOCAL * PAIR_ROWS, HID)
    pair_rows = lax.all_to_all(pairs, "local", 0, 0, tiled=True)
    packed = call(
        pack_kernel,
        [jax.ShapeDtypeStruct((OUT_ROWS, LANE), bf16)] * GROUP,
        route,
        layer_input.T,
        output_grad.T,
    )
    got = [packed[0]] + [from_behind(packed[o], "node", o) for o in range(1, GROUP)]
    shard = jnp.concatenate(got, axis=0).astype(jnp.float16)
    full = lax.all_gather(shard, "local", axis=0, tiled=True).astype(bf16)
    hidden = call(
        hidden_kernel,
        jax.ShapeDtypeStruct((HIDE_ROWS, LANE), bf16),
        full,
        pairs,
        down_weight[0].T,
    )
    spread = lax.all_gather(hidden.astype(jnp.float16), "local", axis=0, tiled=True).astype(bf16)
    summed = call(
        back_kernel, [jax.ShapeDtypeStruct((HOME_ROWS, LANE), bf16)] * GROUP, spread, pair_rows
    )
    home = [summed[0]] + [from_behind(summed[o], "node", -o) for o in range(1, GROUP)]
    input_grad, gate_grad = call(
        unpack_kernel,
        [jax.ShapeDtypeStruct((FEAT, TOK), bf16), jax.ShapeDtypeStruct((2, TOK), f32)],
        route,
        gate_fixed.T,
        *home,
    )
    return input_grad.T, gate_grad.T


def solution(mesh):
    in_specs = (
        P("node", "local"),
        P("node", "local"),
        P("node", None, "local"),
        P("node", None, "local"),
        P("node", "local", None),
        P("node", None),
        P("node", None),
    )
    out_specs = (P("node", "local"), P("node", None))
    return jax.shard_map(body, mesh=mesh, in_specs=in_specs, out_specs=out_specs, check_vma=False)
```

```python
import jax
import jax.numpy as jnp
from jax import lax
from jax.experimental import pallas as pl
from jax.experimental.pallas import tpu as pltpu
from jax.sharding import PartitionSpec as P

GROUP = 4
CAP = 80
TOK = 128
LANE = 128
FEAT = 448
HID = 128
LOCAL = 8
ROUTED = GROUP * CAP
OUT_ROWS = 7 * CAP + 16
HIDE_ROWS = 2 * ROUTED + 16
HOME_ROWS = 4 * CAP + 16
LEVELS = 15
TOKEN_CEILING = 3
HIDDEN_CEILING = 24
GATE_CEILING = 44
INTERPRET = False

f32 = jnp.float32
bf16 = jnp.bfloat16
NT = (((1,), (1,)), ((), ()))
TN = (((0,), (0,)), ((), ()))


def from_behind(value, axis, steps):
    count = lax.axis_size(axis)
    pairs = [(source, (source + steps) % count) for source in range(count)]
    return lax.ppermute(value, axis, pairs)


def tables(route):
    offsets = lax.broadcasted_iota(jnp.int32, (8, TOK), 0)
    first = jnp.broadcast_to(route[0:1], (8, TOK)) == offsets
    second = jnp.broadcast_to(route[1:2], (8, TOK)) == offsets
    chosen = jnp.where(first | second, 1.0, 0.0)
    before = lax.broadcasted_iota(jnp.int32, (TOK, TOK), 0) < lax.broadcasted_iota(jnp.int32, (TOK, TOK), 1)
    ranks = jnp.dot(chosen.astype(bf16), jnp.where(before, 1.0, 0.0).astype(bf16), preferred_element_type=f32)
    ranks = jnp.where(chosen > 0.5, ranks, -1.0)
    slots = lax.broadcasted_iota(jnp.int32, (CAP, TOK), 0).astype(f32)
    return [
        jnp.where(slots == jnp.broadcast_to(ranks[o : o + 1], (CAP, TOK)), 1.0, 0.0).astype(bf16)
        for o in range(GROUP)
    ]


def level_of(top, ceiling):
    level = jnp.zeros_like(top)
    for step in range(1, LEVELS):
        level = level + jnp.where(top < 2.0 ** (ceiling - 8 * step), 1.0, 0.0)
    return level


def power_of(level, ceiling, sign):
    base = 15 - ceiling
    power = jnp.full_like(level, 2.0 ** (sign * base))
    for step in range(1, LEVELS):
        power = jnp.where(level > step - 0.5, 2.0 ** (sign * (base + 8 * step)), power)
    return power


def level_for(wide, ceiling):
    top = jnp.max(jnp.max(jnp.abs(wide), axis=0, keepdims=True), axis=1, keepdims=True)
    return level_of(jnp.broadcast_to(top, (1, LANE)), ceiling)


def scaled(values, ceiling):
    wide = values.astype(f32)
    level = level_for(wide, ceiling)
    return (wide * power_of(level, ceiling, 1)).astype(bf16), level


def pack_kernel(route_ref, in_ref, grad_ref, *out_refs):
    table = jnp.concatenate(tables(route_ref[...]), axis=0)
    rows_in, level_in = scaled(in_ref[...], TOKEN_CEILING)
    rows_grad, level_grad = scaled(grad_ref[...], TOKEN_CEILING)
    tail = jnp.concatenate([rows_in[384:448], rows_grad[384:448]], axis=0)
    parts = [rows_in[0:128], rows_in[128:256], rows_in[256:384]]
    parts += [rows_grad[0:128], rows_grad[128:256], rows_grad[256:384], tail]
    for place, part in enumerate(parts):
        packed = lax.dot_general(table, part, NT, preferred_element_type=f32).astype(bf16)
        for o in range(GROUP):
            out_refs[o][place * CAP : (place + 1) * CAP, :] = packed[o * CAP : (o + 1) * CAP]
    line = lax.broadcasted_iota(jnp.int32, (16, LANE), 0)
    levels = jnp.where(line == 0, level_in, jnp.where(line == 1, level_grad, 0.0)).astype(bf16)
    for o in range(GROUP):
        out_refs[o][7 * CAP : OUT_ROWS, :] = levels


def hidden_kernel(got_ref, gate_ref, up_ref, down_ref, out_ref):
    zero_cols = jnp.zeros((64, 2 * HID), bf16)
    zero_half = jnp.zeros((64, HID), bf16)
    pre = jnp.zeros((ROUTED, 2 * HID), f32)
    grad = jnp.zeros((ROUTED, HID), f32)

    def rows_of(d, o, place):
        start = d * GROUP * OUT_ROWS + o * OUT_ROWS + place * CAP
        return got_ref[start : start + CAP, :]

    def column(d, place):
        return jnp.concatenate([rows_of(d, o, place) for o in range(GROUP)], axis=0)

    for d in range(LOCAL):
        low = d * FEAT
        tail = column(d, 6)
        in_a = jnp.concatenate([column(d, 0), column(d, 1)], axis=1)
        in_b = jnp.concatenate([column(d, 2), tail], axis=1)
        grad_a = jnp.concatenate([column(d, 3), column(d, 4)], axis=1)
        grad_b = jnp.concatenate([column(d, 5), tail], axis=1)
        both = jnp.concatenate([gate_ref[low : low + FEAT, :], up_ref[low : low + FEAT, :]], axis=1)
        down = down_ref[low : low + FEAT, :]
        both_b = jnp.concatenate([both[256:448], zero_cols], axis=0)
        down_b = jnp.concatenate([down[256:384], zero_half, down[384:448]], axis=0)
        part = jnp.dot(in_a, both[0:256], preferred_element_type=f32)
        part = part + jnp.dot(in_b, both_b, preferred_element_type=f32)
        part_grad = jnp.dot(grad_a, down[0:256], preferred_element_type=f32)
        part_grad = part_grad + jnp.dot(grad_b, down_b, preferred_element_type=f32)
        back_in = []
        back_grad = []
        for o in range(GROUP):
            start = d * GROUP * OUT_ROWS + o * OUT_ROWS + 7 * CAP
            levels = got_ref[start : start + 16, :].astype(f32)
            inverse_in = power_of(levels[0:1], TOKEN_CEILING, -1)
            inverse_grad = power_of(levels[1:2], TOKEN_CEILING, -1)
            back_in.append(part[o * CAP : (o + 1) * CAP] * jnp.concatenate([inverse_in, inverse_in], axis=1))
            back_grad.append(part_grad[o * CAP : (o + 1) * CAP] * inverse_grad)
        pre = pre + jnp.concatenate(back_in, axis=0)
        grad = grad + jnp.concatenate(back_grad, axis=0)
    gate_pre = pre[:, 0:HID]
    up_pre = pre[:, HID : 2 * HID]
    sigmoid = jax.nn.sigmoid(gate_pre)
    swish = gate_pre * sigmoid
    product = swish * up_pre * grad
    up_grad, level_up = scaled((grad * swish).astype(bf16), HIDDEN_CEILING)
    pre_grad, level_pre = scaled(
        (grad * up_pre * sigmoid * (1.0 + gate_pre * (1.0 - sigmoid))).astype(bf16), HIDDEN_CEILING
    )
    totals = []
    for o in range(GROUP):
        piece = jnp.concatenate([product[o * CAP : (o + 1) * CAP], jnp.zeros((LANE - CAP, HID), f32)], axis=0)
        total = lax.dot_general(
            jnp.ones((8, HID), f32), piece, NT, preferred_element_type=f32, precision=lax.Precision.HIGHEST
        )
        totals.append(total[0:1])
    level_gate = level_for(jnp.concatenate(totals, axis=0), GATE_CEILING)
    power_gate = power_of(level_gate, GATE_CEILING, 1)
    line = lax.broadcasted_iota(jnp.int32, (16, LANE), 0)
    rows = jnp.where(line == 8, level_pre, jnp.where(line == 9, level_up, jnp.where(line == 10, level_gate, 0.0)))
    for o in range(GROUP):
        total = totals[o] * power_gate
        high = total.astype(bf16).astype(f32)
        rows = jnp.where(line == 2 * o, high, jnp.where(line == 2 * o + 1, total - high, rows))
    out_ref[0:ROUTED, :] = pre_grad
    out_ref[ROUTED : 2 * ROUTED, :] = up_grad
    out_ref[2 * ROUTED : HIDE_ROWS, :] = rows.astype(bf16)


def back_kernel(got_ref, gate_ref, up_ref, *out_refs):
    zero_cols = jnp.zeros((64, 2 * HID), bf16)
    head = jnp.zeros((ROUTED, 384), f32)
    tail = jnp.zeros((2 * CAP, LANE), f32)
    gates = jnp.zeros((16, LANE), f32)
    for d in range(LOCAL):
        base = d * HIDE_ROWS
        rows = got_ref[base + 2 * ROUTED : base + HIDE_ROWS, :].astype(f32)
        inverse_pre = power_of(rows[8:9], HIDDEN_CEILING, -1)
        inverse_up = power_of(rows[9:10], HIDDEN_CEILING, -1)
        gates = gates + rows * power_of(rows[10:11], GATE_CEILING, -1)
        pre_grad = (got_ref[base : base + ROUTED, :].astype(f32) * inverse_pre).astype(bf16)
        up_grad = (got_ref[base + ROUTED : base + 2 * ROUTED, :].astype(f32) * inverse_up).astype(bf16)
        hidden = jnp.concatenate([pre_grad, up_grad], axis=1)
        paired = jnp.concatenate([hidden[0 : 2 * CAP], hidden[2 * CAP : 4 * CAP]], axis=1)
        low = d * FEAT
        both = jnp.concatenate([gate_ref[low : low + FEAT, :], up_ref[low : low + FEAT, :]], axis=1)
        head = head + lax.dot_general(hidden, both[0:384], NT, preferred_element_type=f32)
        corner = jnp.concatenate([both[384:448], zero_cols], axis=1)
        other = jnp.concatenate([zero_cols, both[384:448]], axis=1)
        ends = jnp.concatenate([corner, other], axis=0)
        tail = tail + lax.dot_general(paired, ends, NT, preferred_element_type=f32)
    head = head.astype(bf16)
    tail = tail.astype(bf16)
    line = lax.broadcasted_iota(jnp.int32, (16, LANE), 0)
    for o in range(GROUP):
        for j in range(3):
            out_refs[o][j * CAP : (j + 1) * CAP, :] = head[o * CAP : (o + 1) * CAP, j * LANE : (j + 1) * LANE]
        half = o % 2
        out_refs[o][3 * CAP : 4 * CAP, :] = tail[half * CAP : (half + 1) * CAP]
        gate = gates[2 * o : 2 * o + 1] + gates[2 * o + 1 : 2 * o + 2]
        high = gate.astype(bf16).astype(f32)
        rows = jnp.where(line == 0, high, jnp.where(line == 1, gate - high, 0.0))
        out_refs[o][4 * CAP : HOME_ROWS, :] = rows.astype(bf16)


def unpack_kernel(route_ref, fixed_ref, *refs):
    got_refs = refs[0:GROUP]
    out_ref, gate_ref = refs[GROUP], refs[GROUP + 1]
    route = route_ref[...]
    weights = fixed_ref[...].astype(f32) / 65536.0
    table = tables(route)
    head = jnp.zeros((384, TOK), f32)
    tail = jnp.zeros((64, TOK), f32)
    gate = jnp.zeros((2, TOK), f32)
    for o in range(GROUP):
        got = got_refs[o]
        hits = route == o
        weight = jnp.sum(jnp.where(hits, weights, 0.0), axis=0, keepdims=True)
        rows = jnp.concatenate([got[j * CAP : (j + 1) * CAP, :] for j in range(4)], axis=1)
        back = lax.dot_general(rows, table[o], TN, preferred_element_type=f32)
        head = head + weight * back[0:384]
        tail = tail + weight * (back[384:448] if o < 2 else back[448:512])
        gates = jnp.dot(got[4 * CAP : HOME_ROWS, 0:CAP], table[o], preferred_element_type=f32)
        gate = gate + jnp.where(hits, gates[0:1] + gates[1:2], 0.0)
    out_ref[0:384, :] = head.astype(bf16)
    out_ref[384:448, :] = tail.astype(bf16)
    gate_ref[...] = gate


def call(kernel, outs, *args):
    return pl.pallas_call(kernel, out_shape=outs, interpret=INTERPRET, compiler_params=pltpu.CompilerParams(vmem_limit_bytes=24 * 1024 * 1024))(*args)


def body(layer_input, output_grad, gate_weight, up_weight, down_weight, route_offset, gate_fixed):
    route = route_offset.T
    gate_rows = lax.all_to_all(gate_weight[0], "local", 0, 0, tiled=True)
    packed = call(
        pack_kernel,
        [jax.ShapeDtypeStruct((OUT_ROWS, LANE), bf16)] * GROUP,
        route,
        layer_input.T,
        output_grad.T,
    )
    got = [packed[0]] + [from_behind(packed[o], "node", o) for o in range(1, GROUP)]
    shard = jnp.concatenate(got, axis=0).astype(jnp.float16)
    shard, down_cols = lax.optimization_barrier((shard, down_weight[0].T))
    full, late_up = lax.optimization_barrier((lax.all_gather(shard, "local", axis=0, tiled=True), up_weight[0]))
    full = full.astype(bf16)
    up_rows = lax.all_to_all(late_up, "local", 0, 0, tiled=True)
    hidden = call(
        hidden_kernel,
        jax.ShapeDtypeStruct((HIDE_ROWS, LANE), bf16),
        full,
        gate_weight[0],
        up_weight[0],
        down_cols,
    )
    spread = lax.all_gather(hidden.astype(jnp.float16), "local", axis=0, tiled=True).astype(bf16)
    summed = call(
        back_kernel, [jax.ShapeDtypeStruct((HOME_ROWS, LANE), bf16)] * GROUP, spread, gate_rows, up_rows
    )
    home = [summed[0]] + [from_behind(summed[o], "node", -o) for o in range(1, GROUP)]
    input_grad, gate_grad = call(
        unpack_kernel,
        [jax.ShapeDtypeStruct((FEAT, TOK), bf16), jax.ShapeDtypeStruct((2, TOK), f32)],
        route,
        gate_fixed.T,
        *home,
    )
    return input_grad.T, gate_grad.T


def solution(mesh):
    in_specs = (
        P("node", "local"),
        P("node", "local"),
        P("node", None, "local"),
        P("node", None, "local"),
        P("node", "local", None),
        P("node", None),
        P("node", None),
    )
    out_specs = (P("node", "local"), P("node", None))
    return jax.shard_map(body, mesh=mesh, in_specs=in_specs, out_specs=out_specs, check_vma=False)
```

```python
import jax
import jax.numpy as jnp
from jax import lax
from jax.experimental import pallas as pl
from jax.experimental.pallas import tpu as pltpu
from jax.sharding import PartitionSpec as P

GROUP = 4
CAP = 80
TOK = 128
LANE = 128
FEAT = 448
HID = 128
LOCAL = 8
ROUTED = GROUP * CAP
OUT_ROWS = 7 * CAP + 16
PART_ROWS = 3 * ROUTED + 2 * CAP + 16
HOME_ROWS = 4 * CAP + 16
HIDE_ROWS = 2 * ROUTED + 16
SHARES = LOCAL // 2
HALF_ROWS = SHARES * FEAT
LEVELS = 15
INTERPRET = False

f32 = jnp.float32
bf16 = jnp.bfloat16
NT = (((1,), (1,)), ((), ()))
TN = (((0,), (0,)), ((), ()))


def from_behind(value, axis, steps):
    count = lax.axis_size(axis)
    pairs = [(source, (source + steps) % count) for source in range(count)]
    return lax.ppermute(value, axis, pairs)


def swap(value):
    nodes, count = lax.axis_size("node"), lax.axis_size("local")
    pairs = []
    for node in range(nodes):
        for place in range(count):
            step = 1 if place % 2 == node % 2 else -1
            pairs.append((node * count + place, node * count + (place + step) % count))
    return lax.ppermute(value, ("node", "local"), pairs)


def half_of(weight, parity):
    rows = weight.reshape(SHARES, 2, FEAT, HID)
    return lax.dynamic_index_in_dim(rows, parity, 1, keepdims=False).reshape(HALF_ROWS, HID)


def tables(route):
    offsets = lax.broadcasted_iota(jnp.int32, (8, TOK), 0)
    first = jnp.broadcast_to(route[0:1], (8, TOK)) == offsets
    second = jnp.broadcast_to(route[1:2], (8, TOK)) == offsets
    chosen = jnp.where(first | second, 1.0, 0.0)
    before = lax.broadcasted_iota(jnp.int32, (TOK, TOK), 0) < lax.broadcasted_iota(jnp.int32, (TOK, TOK), 1)
    ranks = jnp.dot(chosen.astype(bf16), jnp.where(before, 1.0, 0.0).astype(bf16), preferred_element_type=f32)
    ranks = jnp.where(chosen > 0.5, ranks, -1.0)
    slots = lax.broadcasted_iota(jnp.int32, (CAP, TOK), 0).astype(f32)
    return [
        jnp.where(slots == jnp.broadcast_to(ranks[o : o + 1], (CAP, TOK)), 1.0, 0.0).astype(bf16)
        for o in range(GROUP)
    ]


def level_of(top):
    level = jnp.zeros_like(top)
    for step in range(1, LEVELS):
        level = level + jnp.where(top < 2.0 ** (3 - 8 * step), 1.0, 0.0)
    return level


def power_of(level, sign):
    power = jnp.full_like(level, 2.0 ** (sign * 12))
    for step in range(1, LEVELS):
        power = jnp.where(level > step - 0.5, 2.0 ** (sign * (12 + 8 * step)), power)
    return power


def scaled(values):
    wide = values.astype(f32)
    top = jnp.max(jnp.max(jnp.abs(wide), axis=0, keepdims=True), axis=1, keepdims=True)
    level = level_of(jnp.broadcast_to(top, (1, TOK)))
    return (wide * power_of(level, 1)).astype(bf16), level


def pack_kernel(route_ref, in_ref, grad_ref, *out_refs):
    table = jnp.concatenate(tables(route_ref[...]), axis=0)
    rows_in, level_in = scaled(in_ref[...])
    rows_grad, level_grad = scaled(grad_ref[...])
    tail = jnp.concatenate([rows_in[384:448], rows_grad[384:448]], axis=0)
    parts = [rows_in[0:128], rows_in[128:256], rows_in[256:384]]
    parts += [rows_grad[0:128], rows_grad[128:256], rows_grad[256:384], tail]
    for place, part in enumerate(parts):
        packed = lax.dot_general(table, part, NT, preferred_element_type=f32).astype(bf16)
        for o in range(GROUP):
            out_refs[o][place * CAP : (place + 1) * CAP, :] = packed[o * CAP : (o + 1) * CAP]
    line = lax.broadcasted_iota(jnp.int32, (16, LANE), 0)
    levels = jnp.where(line == 0, level_in, jnp.where(line == 1, level_grad, 0.0)).astype(bf16)
    for o in range(GROUP):
        out_refs[o][7 * CAP : OUT_ROWS, :] = levels


def hidden_kernel(got_ref, gate_ref, up_ref, down_ref, out_ref):
    zero_cols = jnp.zeros((64, 2 * HID), bf16)
    zero_half = jnp.zeros((64, HID), bf16)
    pre = jnp.zeros((ROUTED, 2 * HID), f32)
    grad = jnp.zeros((ROUTED, HID), f32)

    def rows_of(d, o, place):
        start = d * GROUP * OUT_ROWS + o * OUT_ROWS + place * CAP
        return got_ref[start : start + CAP, :]

    def column(d, place):
        return jnp.concatenate([rows_of(d, o, place) for o in range(GROUP)], axis=0)

    for d in range(LOCAL):
        low = d * FEAT
        tail = column(d, 6)
        in_a = jnp.concatenate([column(d, 0), column(d, 1)], axis=1)
        in_b = jnp.concatenate([column(d, 2), tail], axis=1)
        grad_a = jnp.concatenate([column(d, 3), column(d, 4)], axis=1)
        grad_b = jnp.concatenate([column(d, 5), tail], axis=1)
        both = jnp.concatenate([gate_ref[low : low + FEAT, :], up_ref[low : low + FEAT, :]], axis=1)
        down = down_ref[low : low + FEAT, :]
        both_b = jnp.concatenate([both[256:448], zero_cols], axis=0)
        down_b = jnp.concatenate([down[256:384], zero_half, down[384:448]], axis=0)
        part = jnp.dot(in_a, both[0:256], preferred_element_type=f32)
        part = part + jnp.dot(in_b, both_b, preferred_element_type=f32)
        part_grad = jnp.dot(grad_a, down[0:256], preferred_element_type=f32)
        part_grad = part_grad + jnp.dot(grad_b, down_b, preferred_element_type=f32)
        back_in = []
        back_grad = []
        for o in range(GROUP):
            start = d * GROUP * OUT_ROWS + o * OUT_ROWS + 7 * CAP
            levels = got_ref[start : start + 16, :].astype(f32)
            inverse_in = power_of(levels[0:1], -1)
            inverse_grad = power_of(levels[1:2], -1)
            back_in.append(part[o * CAP : (o + 1) * CAP] * jnp.concatenate([inverse_in, inverse_in], axis=1))
            back_grad.append(part_grad[o * CAP : (o + 1) * CAP] * inverse_grad)
        pre = pre + jnp.concatenate(back_in, axis=0)
        grad = grad + jnp.concatenate(back_grad, axis=0)
    gate_pre = pre[:, 0:HID]
    up_pre = pre[:, HID : 2 * HID]
    sigmoid = jax.nn.sigmoid(gate_pre)
    swish = gate_pre * sigmoid
    product = swish * up_pre * grad
    up_grad = (grad * swish).astype(bf16)
    pre_grad = (grad * up_pre * sigmoid * (1.0 + gate_pre * (1.0 - sigmoid))).astype(bf16)
    line = lax.broadcasted_iota(jnp.int32, (16, LANE), 0)
    gate_rows = jnp.zeros((16, LANE), f32)
    for o in range(GROUP):
        piece = jnp.concatenate([product[o * CAP : (o + 1) * CAP], jnp.zeros((LANE - CAP, HID), f32)], axis=0)
        total = lax.dot_general(
            jnp.ones((8, HID), f32), piece, NT, preferred_element_type=f32, precision=lax.Precision.HIGHEST
        )[0:1]
        gate_rows = with_gate(gate_rows, line, o, total)
    out_ref[0:ROUTED, :] = pre_grad
    out_ref[ROUTED : 2 * ROUTED, :] = up_grad
    out_ref[2 * ROUTED : HIDE_ROWS, :] = gate_rows.astype(bf16)


def with_gate(rows, line, o, total):
    high = total.astype(bf16).astype(f32)
    return jnp.where(line == 2 * o, high, jnp.where(line == 2 * o + 1, total - high, rows))


def back_kernel(own_ref, other_ref, own_gate_ref, own_up_ref, other_ref_rows, out_ref):
    zero_cols = jnp.zeros((64, 4 * HID), bf16)
    hidden = jnp.concatenate(
        [
            own_ref[0:ROUTED, :],
            own_ref[ROUTED : 2 * ROUTED, :],
            other_ref[0:ROUTED, :],
            other_ref[ROUTED : 2 * ROUTED, :],
        ],
        axis=1,
    )
    paired = jnp.concatenate([hidden[0 : 2 * CAP], hidden[2 * CAP : 4 * CAP]], axis=1)
    own_gates = own_ref[2 * ROUTED : HIDE_ROWS, :].astype(f32)
    other_gates = other_ref[2 * ROUTED : HIDE_ROWS, :].astype(f32)
    line = lax.broadcasted_iota(jnp.int32, (16, LANE), 0)
    gate_rows = jnp.zeros((16, LANE), f32)
    for o in range(GROUP):
        own = own_gates[2 * o : 2 * o + 1] + own_gates[2 * o + 1 : 2 * o + 2]
        other = other_gates[2 * o : 2 * o + 1] + other_gates[2 * o + 1 : 2 * o + 2]
        gate_rows = with_gate(gate_rows, line, o, own + other)
    gate_rows = gate_rows.astype(bf16)
    for d in range(SHARES):
        low = d * FEAT
        base = d * PART_ROWS
        weights = jnp.concatenate(
            [
                own_gate_ref[low : low + FEAT, :],
                own_up_ref[low : low + FEAT, :],
                other_ref_rows[low : low + FEAT, :],
                other_ref_rows[HALF_ROWS + low : HALF_ROWS + low + FEAT, :],
            ],
            axis=1,
        )
        wide = lax.dot_general(hidden, weights[0:384], NT, preferred_element_type=f32).astype(bf16)
        for j in range(3):
            out_ref[base + j * ROUTED : base + (j + 1) * ROUTED, :] = wide[:, j * LANE : (j + 1) * LANE]
        corner = jnp.concatenate([weights[384:448], zero_cols], axis=1)
        other = jnp.concatenate([zero_cols, weights[384:448]], axis=1)
        ends = jnp.concatenate([corner, other], axis=0)
        tail = lax.dot_general(paired, ends, NT, preferred_element_type=f32).astype(bf16)
        out_ref[base + 3 * ROUTED : base + 3 * ROUTED + 2 * CAP, :] = tail
        out_ref[base + 3 * ROUTED + 2 * CAP : base + PART_ROWS, :] = gate_rows


def sum_kernel(part_ref, *out_refs):
    def total(start, rows):
        value = part_ref[start : start + rows, :].astype(f32)
        for d in range(1, SHARES):
            value = value + part_ref[d * PART_ROWS + start : d * PART_ROWS + start + rows, :].astype(f32)
        return value

    for j in range(3):
        for o in range(GROUP):
            out_refs[o][j * CAP : (j + 1) * CAP, :] = total(j * ROUTED + o * CAP, CAP).astype(bf16)
    for half in range(2):
        tail = total(3 * ROUTED + half * CAP, CAP).astype(bf16)
        out_refs[half][3 * CAP : 4 * CAP, :] = tail
        out_refs[half + 2][3 * CAP : 4 * CAP, :] = tail
    gates = total(3 * ROUTED + 2 * CAP, 16)
    line = lax.broadcasted_iota(jnp.int32, (16, LANE), 0)
    for o in range(GROUP):
        gate = gates[2 * o : 2 * o + 1] + gates[2 * o + 1 : 2 * o + 2]
        high = gate.astype(bf16).astype(f32)
        rows = jnp.where(line == 0, high, jnp.where(line == 1, gate - high, 0.0))
        out_refs[o][4 * CAP : HOME_ROWS, :] = rows.astype(bf16)


def unpack_kernel(route_ref, fixed_ref, *refs):
    got_refs = refs[0:GROUP]
    out_ref, gate_ref = refs[GROUP], refs[GROUP + 1]
    route = route_ref[...]
    weights = fixed_ref[...].astype(f32) / 65536.0
    table = tables(route)
    head = jnp.zeros((384, TOK), f32)
    tail = jnp.zeros((64, TOK), f32)
    gate = jnp.zeros((2, TOK), f32)
    for o in range(GROUP):
        got = got_refs[o]
        hits = route == o
        weight = jnp.sum(jnp.where(hits, weights, 0.0), axis=0, keepdims=True)
        rows = jnp.concatenate([got[j * CAP : (j + 1) * CAP, :] for j in range(4)], axis=1)
        back = lax.dot_general(rows, table[o], TN, preferred_element_type=f32)
        head = head + weight * back[0:384]
        tail = tail + weight * (back[384:448] if o < 2 else back[448:512])
        gates = jnp.dot(got[4 * CAP : HOME_ROWS, 0:CAP], table[o], preferred_element_type=f32)
        gate = gate + jnp.where(hits, gates[0:1] + gates[1:2], 0.0)
    out_ref[0:384, :] = head.astype(bf16)
    out_ref[384:448, :] = tail.astype(bf16)
    gate_ref[...] = gate


def call(kernel, outs, *args):
    return pl.pallas_call(kernel, out_shape=outs, interpret=INTERPRET, compiler_params=pltpu.CompilerParams(vmem_limit_bytes=24 * 1024 * 1024))(*args)


def body(layer_input, output_grad, gate_weight, up_weight, down_weight, route_offset, gate_fixed):
    route = route_offset.T
    parity = lax.axis_index("local") % 2
    other_rows = swap(
        jnp.concatenate([half_of(gate_weight[0], 1 - parity), half_of(up_weight[0], 1 - parity)], axis=0)
    )
    packed = call(
        pack_kernel,
        [jax.ShapeDtypeStruct((OUT_ROWS, LANE), bf16)] * GROUP,
        route,
        layer_input.T,
        output_grad.T,
    )
    got = [packed[0]] + [from_behind(packed[o], "node", o) for o in range(1, GROUP)]
    shard = jnp.concatenate(got, axis=0).astype(jnp.float16)
    shard, down_cols, kept_gate, kept_up = lax.optimization_barrier(
        (shard, down_weight[0].T, half_of(gate_weight[0], parity), half_of(up_weight[0], parity))
    )
    full = lax.all_gather(shard, "local", axis=0, tiled=True).astype(bf16)
    hidden = call(
        hidden_kernel,
        jax.ShapeDtypeStruct((HIDE_ROWS, LANE), bf16),
        full,
        gate_weight[0],
        up_weight[0],
        down_cols,
    )
    other_hidden = swap(hidden)
    partial = call(
        back_kernel,
        jax.ShapeDtypeStruct((SHARES * PART_ROWS, LANE), bf16),
        hidden,
        other_hidden,
        kept_gate,
        kept_up,
        other_rows,
    )
    groups = [[2 * place + odd for place in range(SHARES)] for odd in range(2)]
    shares = lax.all_to_all(partial, "local", 0, 0, tiled=True, axis_index_groups=groups)
    summed = call(sum_kernel, [jax.ShapeDtypeStruct((HOME_ROWS, LANE), bf16)] * GROUP, shares)
    home = [summed[0]] + [from_behind(summed[o], "node", -o) for o in range(1, GROUP)]
    input_grad, gate_grad = call(
        unpack_kernel,
        [jax.ShapeDtypeStruct((FEAT, TOK), bf16), jax.ShapeDtypeStruct((2, TOK), f32)],
        route,
        gate_fixed.T,
        *home,
    )
    return input_grad.T, gate_grad.T


def solution(mesh):
    in_specs = (
        P("node", "local"),
        P("node", "local"),
        P("node", None, "local"),
        P("node", None, "local"),
        P("node", "local", None),
        P("node", None),
        P("node", None),
    )
    out_specs = (P("node", "local"), P("node", None))
    return jax.shard_map(body, mesh=mesh, in_specs=in_specs, out_specs=out_specs, check_vma=False)
```

```python
import jax
import jax.numpy as jnp
from jax import lax
from jax.experimental import pallas as pl
from jax.experimental.pallas import tpu as pltpu
from jax.sharding import PartitionSpec as P

GROUP = 4
CAP = 80
TOK = 128
LANE = 128
FEAT = 448
HID = 128
LOCAL = 8
ROUTED = GROUP * CAP
OUT_ROWS = 7 * CAP + 16
SHARD_ROWS = GROUP * 7 * CAP + 16
PART_ROWS = 3 * ROUTED + 2 * CAP + 16
HOME_ROWS = 4 * CAP + 16
HIDE_ROWS = 2 * ROUTED + 16
SHARES = LOCAL // 2
HALF_ROWS = SHARES * FEAT
LEVELS = 15
INTERPRET = False

f32 = jnp.float32
bf16 = jnp.bfloat16
NT = (((1,), (1,)), ((), ()))
TN = (((0,), (0,)), ((), ()))


def from_behind(value, axis, steps):
    count = lax.axis_size(axis)
    pairs = [(source, (source + steps) % count) for source in range(count)]
    return lax.ppermute(value, axis, pairs)


def beside(core, place):
    return (place + 1 - 2 * ((place + core) & 1)) & 7


def across(core, place):
    return ((((place - 2 * core) & 7) ^ 2) + 2 * core) & 7


def swap(value, partner, turn):
    nodes, count = lax.axis_size("node"), lax.axis_size("local")
    pairs = [
        (node * count + place, node * count + partner((node + turn) & 1, place))
        for node in range(nodes)
        for place in range(count)
    ]
    return lax.ppermute(value, ("node", "local"), pairs)


def targets(core, place):
    return place, across(1 - core, place), across(core, place), (place + 4) & 7


def pick_kernel(where_ref, gate_ref, up_ref, out_ref):
    core = where_ref[0] & 1
    theirs = targets(core, beside(core, where_ref[1]))
    for turn in range(SHARES):
        start = pl.multiple_of(theirs[turn] * FEAT, 64)
        low = turn * FEAT
        out_ref[low : low + FEAT, :] = gate_ref[pl.ds(start, FEAT), :]
        out_ref[HALF_ROWS + low : HALF_ROWS + low + FEAT, :] = up_ref[pl.ds(start, FEAT), :]


def tables(route):
    offsets = lax.broadcasted_iota(jnp.int32, (8, TOK), 0)
    first = jnp.broadcast_to(route[0:1], (8, TOK)) == offsets
    second = jnp.broadcast_to(route[1:2], (8, TOK)) == offsets
    chosen = jnp.where(first | second, 1.0, 0.0)
    before = lax.broadcasted_iota(jnp.int32, (TOK, TOK), 0) < lax.broadcasted_iota(jnp.int32, (TOK, TOK), 1)
    ranks = jnp.dot(chosen.astype(bf16), jnp.where(before, 1.0, 0.0).astype(bf16), preferred_element_type=f32)
    ranks = jnp.where(chosen > 0.5, ranks, -1.0)
    slots = lax.broadcasted_iota(jnp.int32, (CAP, TOK), 0).astype(f32)
    return [
        jnp.where(slots == jnp.broadcast_to(ranks[o : o + 1], (CAP, TOK)), 1.0, 0.0).astype(bf16)
        for o in range(GROUP)
    ]


def level_of(top):
    level = jnp.zeros_like(top)
    for step in range(1, LEVELS):
        level = level + jnp.where(top < 2.0 ** (3 - 8 * step), 1.0, 0.0)
    return level


def power_of(level, sign):
    power = jnp.full_like(level, 2.0 ** (sign * 12))
    for step in range(1, LEVELS):
        power = jnp.where(level > step - 0.5, 2.0 ** (sign * (12 + 8 * step)), power)
    return power


def scaled(values):
    wide = values.astype(f32)
    top = jnp.max(jnp.max(jnp.abs(wide), axis=0, keepdims=True), axis=1, keepdims=True)
    level = level_of(jnp.broadcast_to(top, (1, TOK)))
    return (wide * power_of(level, 1)).astype(bf16), level


def pack_kernel(route_ref, in_ref, grad_ref, *out_refs):
    table = jnp.concatenate(tables(route_ref[...]), axis=0)
    rows_in, level_in = scaled(in_ref[...])
    rows_grad, level_grad = scaled(grad_ref[...])
    tail = jnp.concatenate([rows_in[384:448], rows_grad[384:448]], axis=0)
    parts = [rows_in[0:128], rows_in[128:256], rows_in[256:384]]
    parts += [rows_grad[0:128], rows_grad[128:256], rows_grad[256:384], tail]
    for place, part in enumerate(parts):
        packed = lax.dot_general(table, part, NT, preferred_element_type=f32).astype(bf16)
        for o in range(GROUP):
            out_refs[o][place * CAP : (place + 1) * CAP, :] = packed[o * CAP : (o + 1) * CAP]
    line = lax.broadcasted_iota(jnp.int32, (16, LANE), 0)
    for o in range(GROUP):
        levels = jnp.where(line == 2 * o, level_in, jnp.where(line == 2 * o + 1, level_grad, 0.0))
        out_refs[o][7 * CAP : OUT_ROWS, :] = levels.astype(bf16)


def hidden_kernel(got_ref, gate_ref, up_ref, down_ref, out_ref):
    zero_cols = jnp.zeros((64, 2 * HID), bf16)
    zero_half = jnp.zeros((64, HID), bf16)
    pre = jnp.zeros((ROUTED, 2 * HID), f32)
    grad = jnp.zeros((ROUTED, HID), f32)

    def rows_of(d, o, place):
        start = d * SHARD_ROWS + (o * 7 + place) * CAP
        return got_ref[start : start + CAP, :]

    def column(d, place):
        return jnp.concatenate([rows_of(d, o, place) for o in range(GROUP)], axis=0)

    for d in range(LOCAL):
        low = d * FEAT
        tail = column(d, 6)
        in_a = jnp.concatenate([column(d, 0), column(d, 1)], axis=1)
        in_b = jnp.concatenate([column(d, 2), tail], axis=1)
        grad_a = jnp.concatenate([column(d, 3), column(d, 4)], axis=1)
        grad_b = jnp.concatenate([column(d, 5), tail], axis=1)
        both = jnp.concatenate([gate_ref[low : low + FEAT, :], up_ref[low : low + FEAT, :]], axis=1)
        down = down_ref[low : low + FEAT, :]
        both_b = jnp.concatenate([both[256:448], zero_cols], axis=0)
        down_b = jnp.concatenate([down[256:384], zero_half, down[384:448]], axis=0)
        part = jnp.dot(in_a, both[0:256], preferred_element_type=f32)
        part = part + jnp.dot(in_b, both_b, preferred_element_type=f32)
        part_grad = jnp.dot(grad_a, down[0:256], preferred_element_type=f32)
        part_grad = part_grad + jnp.dot(grad_b, down_b, preferred_element_type=f32)
        back_in = []
        back_grad = []
        levels = got_ref[(d + 1) * SHARD_ROWS - 16 : (d + 1) * SHARD_ROWS, :].astype(f32)
        for o in range(GROUP):
            inverse_in = power_of(levels[2 * o : 2 * o + 1], -1)
            inverse_grad = power_of(levels[2 * o + 1 : 2 * o + 2], -1)
            back_in.append(part[o * CAP : (o + 1) * CAP] * jnp.concatenate([inverse_in, inverse_in], axis=1))
            back_grad.append(part_grad[o * CAP : (o + 1) * CAP] * inverse_grad)
        pre = pre + jnp.concatenate(back_in, axis=0)
        grad = grad + jnp.concatenate(back_grad, axis=0)
    gate_pre = pre[:, 0:HID]
    up_pre = pre[:, HID : 2 * HID]
    sigmoid = jax.nn.sigmoid(gate_pre)
    swish = gate_pre * sigmoid
    product = swish * up_pre * grad
    up_grad = (grad * swish).astype(bf16)
    pre_grad = (grad * up_pre * sigmoid * (1.0 + gate_pre * (1.0 - sigmoid))).astype(bf16)
    line = lax.broadcasted_iota(jnp.int32, (16, LANE), 0)
    gate_rows = jnp.zeros((16, LANE), f32)
    for o in range(GROUP):
        piece = jnp.concatenate([product[o * CAP : (o + 1) * CAP], jnp.zeros((LANE - CAP, HID), f32)], axis=0)
        total = lax.dot_general(
            jnp.ones((8, HID), f32), piece, NT, preferred_element_type=f32, precision=lax.Precision.HIGHEST
        )[0:1]
        gate_rows = with_gate(gate_rows, line, o, total)
    out_ref[0:ROUTED, :] = pre_grad
    out_ref[ROUTED : 2 * ROUTED, :] = up_grad
    out_ref[2 * ROUTED : HIDE_ROWS, :] = gate_rows.astype(bf16)


def with_gate(rows, line, o, total):
    high = total.astype(bf16).astype(f32)
    return jnp.where(line == 2 * o, high, jnp.where(line == 2 * o + 1, total - high, rows))


def back_kernel(where_ref, own_ref, other_ref, own_gate_ref, own_up_ref, other_ref_rows, kept_ref, sent_ref):
    mine = targets(where_ref[0] & 1, where_ref[1])
    zero_cols = jnp.zeros((64, 4 * HID), bf16)
    hidden = jnp.concatenate(
        [
            own_ref[0:ROUTED, :],
            own_ref[ROUTED : 2 * ROUTED, :],
            other_ref[0:ROUTED, :],
            other_ref[ROUTED : 2 * ROUTED, :],
        ],
        axis=1,
    )
    paired = jnp.concatenate([hidden[0 : 2 * CAP], hidden[2 * CAP : 4 * CAP]], axis=1)
    own_gates = own_ref[2 * ROUTED : HIDE_ROWS, :].astype(f32)
    other_gates = other_ref[2 * ROUTED : HIDE_ROWS, :].astype(f32)
    line = lax.broadcasted_iota(jnp.int32, (16, LANE), 0)
    gate_rows = jnp.zeros((16, LANE), f32)
    for o in range(GROUP):
        own = own_gates[2 * o : 2 * o + 1] + own_gates[2 * o + 1 : 2 * o + 2]
        other = other_gates[2 * o : 2 * o + 1] + other_gates[2 * o + 1 : 2 * o + 2]
        gate_rows = with_gate(gate_rows, line, o, own + other)
    for d in range(SHARES):
        low = d * FEAT
        base = d % 2 * PART_ROWS
        out_ref = kept_ref if d < 2 else sent_ref
        kind = f32 if d < 2 else bf16
        start = pl.multiple_of(mine[d] * FEAT, 64)
        weights = jnp.concatenate(
            [
                own_gate_ref[pl.ds(start, FEAT), :],
                own_up_ref[pl.ds(start, FEAT), :],
                other_ref_rows[low : low + FEAT, :],
                other_ref_rows[HALF_ROWS + low : HALF_ROWS + low + FEAT, :],
            ],
            axis=1,
        )
        wide = lax.dot_general(hidden, weights[0:384], NT, preferred_element_type=f32).astype(kind)
        for j in range(3):
            out_ref[base + j * ROUTED : base + (j + 1) * ROUTED, :] = wide[:, j * LANE : (j + 1) * LANE]
        corner = jnp.concatenate([weights[384:448], zero_cols], axis=1)
        other = jnp.concatenate([zero_cols, weights[384:448]], axis=1)
        ends = jnp.concatenate([corner, other], axis=0)
        tail = lax.dot_general(paired, ends, NT, preferred_element_type=f32).astype(kind)
        out_ref[base + 3 * ROUTED : base + 3 * ROUTED + 2 * CAP, :] = tail
        out_ref[base + 3 * ROUTED + 2 * CAP : base + PART_ROWS, :] = gate_rows.astype(kind)


def merge_kernel(kept_ref, got_ref, own_ref, sent_ref):
    last = PART_ROWS - 16
    own_ref[...] = kept_ref[0:PART_ROWS, :] + got_ref[0:PART_ROWS, :].astype(f32)
    sent_ref[0:last, :] = (
        kept_ref[PART_ROWS : PART_ROWS + last, :] + got_ref[PART_ROWS : PART_ROWS + last, :].astype(f32)
    ).astype(bf16)
    gates = kept_ref[PART_ROWS + last :, :] + got_ref[PART_ROWS + last :, :].astype(f32)
    line = lax.broadcasted_iota(jnp.int32, (16, LANE), 0)
    rows = jnp.zeros((16, LANE), f32)
    for o in range(GROUP):
        rows = with_gate(rows, line, o, gates[2 * o : 2 * o + 1] + gates[2 * o + 1 : 2 * o + 2])
    sent_ref[last:PART_ROWS, :] = rows.astype(bf16)


def sum_kernel(own_ref, got_ref, *out_refs):
    def total(start, rows):
        return own_ref[start : start + rows, :] + got_ref[start : start + rows, :].astype(f32)

    for j in range(3):
        for o in range(GROUP):
            out_refs[o][j * CAP : (j + 1) * CAP, :] = total(j * ROUTED + o * CAP, CAP).astype(bf16)
    for half in range(2):
        tail = total(3 * ROUTED + half * CAP, CAP).astype(bf16)
        out_refs[half][3 * CAP : 4 * CAP, :] = tail
        out_refs[half + 2][3 * CAP : 4 * CAP, :] = tail
    gates = total(3 * ROUTED + 2 * CAP, 16)
    line = lax.broadcasted_iota(jnp.int32, (16, LANE), 0)
    for o in range(GROUP):
        gate = gates[2 * o : 2 * o + 1] + gates[2 * o + 1 : 2 * o + 2]
        high = gate.astype(bf16).astype(f32)
        rows = jnp.where(line == 0, high, jnp.where(line == 1, gate - high, 0.0))
        out_refs[o][4 * CAP : HOME_ROWS, :] = rows.astype(bf16)


def unpack_kernel(route_ref, fixed_ref, *refs):
    got_refs = refs[0:GROUP]
    out_ref, gate_ref = refs[GROUP], refs[GROUP + 1]
    route = route_ref[...]
    weights = fixed_ref[...].astype(f32) / 65536.0
    table = tables(route)
    head = jnp.zeros((384, TOK), f32)
    tail = jnp.zeros((64, TOK), f32)
    gate = jnp.zeros((2, TOK), f32)
    for o in range(GROUP):
        got = got_refs[o]
        hits = route == o
        weight = jnp.sum(jnp.where(hits, weights, 0.0), axis=0, keepdims=True)
        rows = jnp.concatenate([got[j * CAP : (j + 1) * CAP, :] for j in range(4)], axis=1)
        back = lax.dot_general(rows, table[o], TN, preferred_element_type=f32)
        head = head + weight * back[0:384]
        tail = tail + weight * (back[384:448] if o < 2 else back[448:512])
        gates = jnp.dot(got[4 * CAP : HOME_ROWS, 0:CAP], table[o], preferred_element_type=f32)
        gate = gate + jnp.where(hits, gates[0:1] + gates[1:2], 0.0)
    out_ref[0:384, :] = head.astype(bf16)
    out_ref[384:448, :] = tail.astype(bf16)
    gate_ref[...] = gate


def call(kernel, outs, *args, scalars=0):
    spaces = [pltpu.SMEM if number < scalars else pltpu.VMEM for number in range(len(args))]
    return pl.pallas_call(
        kernel,
        out_shape=outs,
        in_specs=[pl.BlockSpec(memory_space=space) for space in spaces],
        interpret=INTERPRET,
        compiler_params=pltpu.CompilerParams(vmem_limit_bytes=24 * 1024 * 1024),
    )(*args)


def body(layer_input, output_grad, gate_weight, up_weight, down_weight, route_offset, gate_fixed):
    route = route_offset.T
    where = jnp.stack([lax.axis_index("node"), lax.axis_index("local")])
    picked = call(
        pick_kernel,
        jax.ShapeDtypeStruct((2 * HALF_ROWS, HID), bf16),
        where,
        gate_weight[0],
        up_weight[0],
        scalars=1,
    )
    other_rows = swap(picked, beside, 0)
    packed = call(
        pack_kernel,
        [jax.ShapeDtypeStruct((OUT_ROWS, LANE), bf16)] * GROUP,
        route,
        layer_input.T,
        output_grad.T,
    )
    got = [packed[0]] + [from_behind(packed[o], "node", o) for o in range(1, GROUP)]
    levels = got[0][7 * CAP :] + got[1][7 * CAP :] + got[2][7 * CAP :] + got[3][7 * CAP :]
    shard = jnp.concatenate([value[: 7 * CAP] for value in got] + [levels], axis=0).astype(jnp.float16)
    shard, down_cols = lax.optimization_barrier((shard, down_weight[0].T))
    full = lax.all_gather(shard, "local", axis=0, tiled=True).astype(bf16)
    hidden = call(
        hidden_kernel,
        jax.ShapeDtypeStruct((HIDE_ROWS, LANE), bf16),
        full,
        gate_weight[0],
        up_weight[0],
        down_cols,
    )
    other_hidden = swap(hidden, beside, 0)
    kept, sent = call(
        back_kernel,
        [jax.ShapeDtypeStruct((2 * PART_ROWS, LANE), f32), jax.ShapeDtypeStruct((2 * PART_ROWS, LANE), bf16)],
        where,
        hidden,
        other_hidden,
        gate_weight[0],
        up_weight[0],
        other_rows,
        scalars=1,
    )
    own_share, far_share = call(
        merge_kernel,
        [jax.ShapeDtypeStruct((PART_ROWS, LANE), f32), jax.ShapeDtypeStruct((PART_ROWS, LANE), bf16)],
        kept,
        swap(sent, across, 0),
    )
    summed = call(
        sum_kernel,
        [jax.ShapeDtypeStruct((HOME_ROWS, LANE), bf16)] * GROUP,
        own_share,
        swap(far_share, across, 1),
    )
    home = [summed[0]] + [from_behind(summed[o], "node", -o) for o in range(1, GROUP)]
    input_grad, gate_grad = call(
        unpack_kernel,
        [jax.ShapeDtypeStruct((FEAT, TOK), bf16), jax.ShapeDtypeStruct((2, TOK), f32)],
        route,
        gate_fixed.T,
        *home,
    )
    return input_grad.T, gate_grad.T


def solution(mesh):
    in_specs = (
        P("node", "local"),
        P("node", "local"),
        P("node", None, "local"),
        P("node", None, "local"),
        P("node", "local", None),
        P("node", None),
        P("node", None),
    )
    out_specs = (P("node", "local"), P("node", None))
    return jax.shard_map(body, mesh=mesh, in_specs=in_specs, out_specs=out_specs, check_vma=False)
```

```python
import jax
import jax.numpy as jnp
from jax import lax
from jax.experimental import pallas as pl
from jax.experimental.pallas import tpu as pltpu
from jax.sharding import PartitionSpec as P

GROUP = 4
CAP = 80
TOK = 128
LANE = 128
FEAT = 448
HID = 128
LOCAL = 8
ROUTED = GROUP * CAP
OUT_ROWS = 7 * CAP + 16
SHARD_ROWS = GROUP * 7 * CAP + 16
PART_ROWS = 3 * ROUTED + 2 * CAP + 16
HOME_ROWS = 4 * CAP + 16
HIDE_ROWS = 2 * ROUTED + 16
SHARES = LOCAL // 2
HALF_ROWS = SHARES * FEAT
LEVELS = 15
INTERPRET = False
LIMIT = 10

f32 = jnp.float32
bf16 = jnp.bfloat16
NT = (((1,), (1,)), ((), ()))
TN = (((0,), (0,)), ((), ()))


def from_behind(value, axis, steps):
    count = lax.axis_size(axis)
    pairs = [(source, (source + steps) % count) for source in range(count)]
    return lax.ppermute(value, axis, pairs)


def beside(core, place):
    return (place + 1 - 2 * ((place + core) & 1)) & 7


def across(core, place):
    return ((((place - 2 * core) & 7) ^ 2) + 2 * core) & 7


def swap(value, partner, turn):
    nodes, count = lax.axis_size("node"), lax.axis_size("local")
    pairs = [
        (node * count + place, node * count + partner((node + turn) & 1, place))
        for node in range(nodes)
        for place in range(count)
    ]
    return lax.ppermute(value, ("node", "local"), pairs)


def targets(core, place):
    return place, across(1 - core, place), across(core, place), (place + 4) & 7


def pick_kernel(where_ref, gate_ref, up_ref, out_ref, sems):
    core = where_ref[0] & 1
    theirs = targets(core, beside(core, where_ref[1]))
    copies = []
    for turn in range(SHARES):
        start = pl.multiple_of(theirs[turn] * FEAT, 64)
        for half, ref in enumerate((gate_ref, up_ref)):
            low = half * HALF_ROWS + turn * FEAT
            copies.append(
                pltpu.make_async_copy(
                    ref.at[pl.ds(start, FEAT), :], out_ref.at[low : low + FEAT, :], sems.at[2 * turn + half]
                )
            )
    for copy in copies:
        copy.start()
    for copy in copies:
        copy.wait()


def tables(route):
    offsets = lax.broadcasted_iota(jnp.int32, (8, TOK), 0)
    first = jnp.broadcast_to(route[0:1], (8, TOK)) == offsets
    second = jnp.broadcast_to(route[1:2], (8, TOK)) == offsets
    chosen = jnp.where(first | second, 1.0, 0.0)
    before = lax.broadcasted_iota(jnp.int32, (TOK, TOK), 0) < lax.broadcasted_iota(jnp.int32, (TOK, TOK), 1)
    ranks = jnp.dot(chosen.astype(bf16), jnp.where(before, 1.0, 0.0).astype(bf16), preferred_element_type=f32)
    ranks = jnp.where(chosen > 0.5, ranks, -1.0)
    slots = lax.broadcasted_iota(jnp.int32, (CAP, TOK), 0).astype(f32)
    return [
        jnp.where(slots == jnp.broadcast_to(ranks[o : o + 1], (CAP, TOK)), 1.0, 0.0).astype(bf16)
        for o in range(GROUP)
    ]


def level_of(top):
    level = jnp.zeros_like(top)
    for step in range(1, LEVELS):
        level = level + jnp.where(top < 2.0 ** (3 - 8 * step), 1.0, 0.0)
    return level


def power_of(level, sign):
    power = jnp.full_like(level, 2.0 ** (sign * 12))
    for step in range(1, LEVELS):
        power = jnp.where(level > step - 0.5, 2.0 ** (sign * (12 + 8 * step)), power)
    return power


def scaled(values):
    wide = values.astype(f32)
    top = jnp.max(jnp.max(jnp.abs(wide), axis=0, keepdims=True), axis=1, keepdims=True)
    level = level_of(jnp.broadcast_to(top, (1, TOK)))
    return (wide * power_of(level, 1)).astype(bf16), level


def pack_kernel(route_hbm, in_hbm, grad_hbm, *refs):
    out_refs = refs[0:GROUP]
    route_ref, in_ref, grad_ref, sems = refs[GROUP:]
    copies = [
        pltpu.make_async_copy(source, target, sems.at[number])
        for number, (source, target) in enumerate(((route_hbm, route_ref), (in_hbm, in_ref), (grad_hbm, grad_ref)))
    ]
    for copy in copies:
        copy.start()
    for copy in copies:
        copy.wait()
    table = jnp.concatenate(tables(route_ref[...]), axis=0)
    rows_in, level_in = scaled(in_ref[...])
    rows_grad, level_grad = scaled(grad_ref[...])
    tail = jnp.concatenate([rows_in[384:448], rows_grad[384:448]], axis=0)
    parts = [rows_in[0:128], rows_in[128:256], rows_in[256:384]]
    parts += [rows_grad[0:128], rows_grad[128:256], rows_grad[256:384], tail]
    for place, part in enumerate(parts):
        packed = lax.dot_general(table, part, NT, preferred_element_type=f32).astype(bf16)
        for o in range(GROUP):
            out_refs[o][place * CAP : (place + 1) * CAP, :] = packed[o * CAP : (o + 1) * CAP]
    line = lax.broadcasted_iota(jnp.int32, (16, LANE), 0)
    for o in range(GROUP):
        levels = jnp.where(line == 2 * o, level_in, jnp.where(line == 2 * o + 1, level_grad, 0.0))
        out_refs[o][7 * CAP : OUT_ROWS, :] = levels.astype(bf16)


def join_kernel(*refs):
    out_ref = refs[GROUP]
    levels = jnp.zeros((16, LANE), bf16)
    for o in range(GROUP):
        out_ref[o * 7 * CAP : (o + 1) * 7 * CAP, :] = refs[o][0 : 7 * CAP, :]
        levels = levels + refs[o][7 * CAP : OUT_ROWS, :]
    out_ref[GROUP * 7 * CAP : SHARD_ROWS, :] = levels


def hidden_kernel(got_ref, gate_ref, up_ref, down_ref, out_ref):
    zero_cols = jnp.zeros((64, 2 * HID), bf16)
    zero_half = jnp.zeros((64, HID), bf16)
    pre = jnp.zeros((ROUTED, 2 * HID), f32)
    grad = jnp.zeros((ROUTED, HID), f32)

    def rows_of(d, o, place):
        start = d * SHARD_ROWS + (o * 7 + place) * CAP
        return got_ref[start : start + CAP, :]

    def column(d, place):
        return jnp.concatenate([rows_of(d, o, place) for o in range(GROUP)], axis=0)

    for d in range(LOCAL):
        low = d * FEAT
        tail = column(d, 6)
        in_a = jnp.concatenate([column(d, 0), column(d, 1)], axis=1)
        in_b = jnp.concatenate([column(d, 2), tail], axis=1)
        grad_a = jnp.concatenate([column(d, 3), column(d, 4)], axis=1)
        grad_b = jnp.concatenate([column(d, 5), tail], axis=1)
        both = jnp.concatenate([gate_ref[low : low + FEAT, :], up_ref[low : low + FEAT, :]], axis=1)
        down = down_ref[low : low + FEAT, :]
        both_b = jnp.concatenate([both[256:448], zero_cols], axis=0)
        down_b = jnp.concatenate([down[256:384], zero_half, down[384:448]], axis=0)
        part = jnp.dot(in_a, both[0:256], preferred_element_type=f32)
        part = part + jnp.dot(in_b, both_b, preferred_element_type=f32)
        part_grad = jnp.dot(grad_a, down[0:256], preferred_element_type=f32)
        part_grad = part_grad + jnp.dot(grad_b, down_b, preferred_element_type=f32)
        back_in = []
        back_grad = []
        levels = got_ref[(d + 1) * SHARD_ROWS - 16 : (d + 1) * SHARD_ROWS, :].astype(f32)
        for o in range(GROUP):
            inverse_in = power_of(levels[2 * o : 2 * o + 1], -1)
            inverse_grad = power_of(levels[2 * o + 1 : 2 * o + 2], -1)
            back_in.append(part[o * CAP : (o + 1) * CAP] * jnp.concatenate([inverse_in, inverse_in], axis=1))
            back_grad.append(part_grad[o * CAP : (o + 1) * CAP] * inverse_grad)
        pre = pre + jnp.concatenate(back_in, axis=0)
        grad = grad + jnp.concatenate(back_grad, axis=0)
    gate_pre = pre[:, 0:HID]
    up_pre = pre[:, HID : 2 * HID]
    sigmoid = jax.nn.sigmoid(gate_pre)
    swish = gate_pre * sigmoid
    product = swish * up_pre * grad
    up_grad = (grad * swish).astype(bf16)
    pre_grad = (grad * up_pre * sigmoid * (1.0 + gate_pre * (1.0 - sigmoid))).astype(bf16)
    line = lax.broadcasted_iota(jnp.int32, (16, LANE), 0)
    gate_rows = jnp.zeros((16, LANE), f32)
    for o in range(GROUP):
        piece = jnp.concatenate([product[o * CAP : (o + 1) * CAP], jnp.zeros((LANE - CAP, HID), f32)], axis=0)
        total = lax.dot_general(
            jnp.ones((8, HID), f32), piece, NT, preferred_element_type=f32, precision=lax.Precision.HIGHEST
        )[0:1]
        gate_rows = with_gate(gate_rows, line, o, total)
    out_ref[0:ROUTED, :] = pre_grad
    out_ref[ROUTED : 2 * ROUTED, :] = up_grad
    out_ref[2 * ROUTED : HIDE_ROWS, :] = gate_rows.astype(bf16)


def with_gate(rows, line, o, total):
    high = total.astype(bf16).astype(f32)
    return jnp.where(line == 2 * o, high, jnp.where(line == 2 * o + 1, total - high, rows))


def back_kernel(where_ref, own_ref, other_ref, own_gate_ref, own_up_ref, other_ref_rows, kept_ref, sent_ref):
    mine = targets(where_ref[0] & 1, where_ref[1])
    zero_cols = jnp.zeros((64, 4 * HID), bf16)
    hidden = jnp.concatenate(
        [
            own_ref[0:ROUTED, :],
            own_ref[ROUTED : 2 * ROUTED, :],
            other_ref[0:ROUTED, :],
            other_ref[ROUTED : 2 * ROUTED, :],
        ],
        axis=1,
    )
    paired = jnp.concatenate([hidden[0 : 2 * CAP], hidden[2 * CAP : 4 * CAP]], axis=1)
    own_gates = own_ref[2 * ROUTED : HIDE_ROWS, :].astype(f32)
    other_gates = other_ref[2 * ROUTED : HIDE_ROWS, :].astype(f32)
    line = lax.broadcasted_iota(jnp.int32, (16, LANE), 0)
    gate_rows = jnp.zeros((16, LANE), f32)
    for o in range(GROUP):
        own = own_gates[2 * o : 2 * o + 1] + own_gates[2 * o + 1 : 2 * o + 2]
        other = other_gates[2 * o : 2 * o + 1] + other_gates[2 * o + 1 : 2 * o + 2]
        gate_rows = with_gate(gate_rows, line, o, own + other)
    for d in range(SHARES):
        low = d * FEAT
        base = d % 2 * PART_ROWS
        out_ref = kept_ref if d < 2 else sent_ref
        kind = f32 if d < 2 else bf16
        start = pl.multiple_of(mine[d] * FEAT, 64)
        weights = jnp.concatenate(
            [
                own_gate_ref[pl.ds(start, FEAT), :],
                own_up_ref[pl.ds(start, FEAT), :],
                other_ref_rows[low : low + FEAT, :],
                other_ref_rows[HALF_ROWS + low : HALF_ROWS + low + FEAT, :],
            ],
            axis=1,
        )
        wide = lax.dot_general(hidden, weights[0:384], NT, preferred_element_type=f32).astype(kind)
        for j in range(3):
            out_ref[base + j * ROUTED : base + (j + 1) * ROUTED, :] = wide[:, j * LANE : (j + 1) * LANE]
        corner = jnp.concatenate([weights[384:448], zero_cols], axis=1)
        other = jnp.concatenate([zero_cols, weights[384:448]], axis=1)
        ends = jnp.concatenate([corner, other], axis=0)
        tail = lax.dot_general(paired, ends, NT, preferred_element_type=f32).astype(kind)
        out_ref[base + 3 * ROUTED : base + 3 * ROUTED + 2 * CAP, :] = tail
        out_ref[base + 3 * ROUTED + 2 * CAP : base + PART_ROWS, :] = gate_rows.astype(kind)


def merge_kernel(kept_ref, got_ref, own_ref, sent_ref):
    last = PART_ROWS - 16
    own_ref[...] = kept_ref[0:PART_ROWS, :] + got_ref[0:PART_ROWS, :].astype(f32)
    sent_ref[0:last, :] = (
        kept_ref[PART_ROWS : PART_ROWS + last, :] + got_ref[PART_ROWS : PART_ROWS + last, :].astype(f32)
    ).astype(bf16)
    gates = kept_ref[PART_ROWS + last :, :] + got_ref[PART_ROWS + last :, :].astype(f32)
    line = lax.broadcasted_iota(jnp.int32, (16, LANE), 0)
    rows = jnp.zeros((16, LANE), f32)
    for o in range(GROUP):
        rows = with_gate(rows, line, o, gates[2 * o : 2 * o + 1] + gates[2 * o + 1 : 2 * o + 2])
    sent_ref[last:PART_ROWS, :] = rows.astype(bf16)


def sum_kernel(own_ref, got_ref, *out_refs):
    def total(start, rows):
        return own_ref[start : start + rows, :] + got_ref[start : start + rows, :].astype(f32)

    for j in range(3):
        for o in range(GROUP):
            out_refs[o][j * CAP : (j + 1) * CAP, :] = total(j * ROUTED + o * CAP, CAP).astype(bf16)
    for half in range(2):
        tail = total(3 * ROUTED + half * CAP, CAP).astype(bf16)
        out_refs[half][3 * CAP : 4 * CAP, :] = tail
        out_refs[half + 2][3 * CAP : 4 * CAP, :] = tail
    gates = total(3 * ROUTED + 2 * CAP, 16)
    line = lax.broadcasted_iota(jnp.int32, (16, LANE), 0)
    for o in range(GROUP):
        gate = gates[2 * o : 2 * o + 1] + gates[2 * o + 1 : 2 * o + 2]
        high = gate.astype(bf16).astype(f32)
        rows = jnp.where(line == 0, high, jnp.where(line == 1, gate - high, 0.0))
        out_refs[o][4 * CAP : HOME_ROWS, :] = rows.astype(bf16)


def unpack_kernel(route_ref, fixed_ref, *refs):
    got_refs = refs[0:GROUP]
    out_ref, gate_ref = refs[GROUP], refs[GROUP + 1]
    route = route_ref[...]
    weights = fixed_ref[...].astype(f32) / 65536.0
    table = tables(route)
    head = jnp.zeros((384, TOK), f32)
    tail = jnp.zeros((64, TOK), f32)
    gate = jnp.zeros((2, TOK), f32)
    for o in range(GROUP):
        got = got_refs[o]
        hits = route == o
        weight = jnp.sum(jnp.where(hits, weights, 0.0), axis=0, keepdims=True)
        rows = jnp.concatenate([got[j * CAP : (j + 1) * CAP, :] for j in range(4)], axis=1)
        back = lax.dot_general(rows, table[o], TN, preferred_element_type=f32)
        head = head + weight * back[0:384]
        tail = tail + weight * (back[384:448] if o < 2 else back[448:512])
        gates = jnp.dot(got[4 * CAP : HOME_ROWS, 0:CAP], table[o], preferred_element_type=f32)
        gate = gate + jnp.where(hits, gates[0:1] + gates[1:2], 0.0)
    out_ref[0:384, :] = head.astype(bf16)
    out_ref[384:448, :] = tail.astype(bf16)
    gate_ref[...] = gate


def call(kernel, outs, *args, scalars=0, far=0, scratch=()):
    spaces = [pltpu.SMEM] * scalars + [pltpu.HBM] * far
    spaces += [pltpu.VMEM] * (len(args) - len(spaces))
    many = isinstance(outs, list)
    if not INTERPRET:
        args = [a if s is pltpu.SMEM else pltpu.with_memory_space_constraint(a, s) for a, s in zip(args, spaces)]
    return pl.pallas_call(
        kernel,
        out_shape=outs,
        in_specs=[pl.BlockSpec(memory_space=space) for space in spaces],
        out_specs=[pl.BlockSpec(memory_space=pltpu.VMEM)] * len(outs) if many else pl.BlockSpec(memory_space=pltpu.VMEM),
        scratch_shapes=list(scratch),
        interpret=INTERPRET,
        compiler_params=pltpu.CompilerParams(vmem_limit_bytes=LIMIT * 1024 * 1024),
    )(*args)


def body(layer_input, output_grad, gate_weight, up_weight, down_weight, route_offset, gate_fixed):
    route = route_offset.T
    where = jnp.stack([lax.axis_index("node"), lax.axis_index("local")])
    picked = call(
        pick_kernel,
        jax.ShapeDtypeStruct((2 * HALF_ROWS, HID), bf16),
        where,
        gate_weight[0],
        up_weight[0],
        scalars=1,
        far=2,
        scratch=[pltpu.SemaphoreType.DMA((2 * SHARES,))],
    )
    other_rows = swap(picked, beside, 0)
    packed = call(
        pack_kernel,
        [jax.ShapeDtypeStruct((OUT_ROWS, LANE), bf16)] * GROUP,
        route,
        layer_input.T,
        output_grad.T,
        far=3,
        scratch=[
            pltpu.VMEM((2, TOK), jnp.int32),
            pltpu.VMEM((FEAT, TOK), bf16),
            pltpu.VMEM((FEAT, TOK), bf16),
            pltpu.SemaphoreType.DMA((3,)),
        ],
    )
    got = [packed[0]] + [from_behind(packed[o], "node", o) for o in range(1, GROUP)]
    got, down_cols = lax.optimization_barrier((got, down_weight[0].T))
    shard = call(join_kernel, jax.ShapeDtypeStruct((SHARD_ROWS, LANE), bf16), *got).astype(jnp.float16)
    full = lax.all_gather(shard, "local", axis=0, tiled=True).astype(bf16)
    hidden = call(
        hidden_kernel,
        jax.ShapeDtypeStruct((HIDE_ROWS, LANE), bf16),
        full,
        gate_weight[0],
        up_weight[0],
        down_cols,
    )
    other_hidden = swap(hidden, beside, 0)
    kept, sent = call(
        back_kernel,
        [jax.ShapeDtypeStruct((2 * PART_ROWS, LANE), f32), jax.ShapeDtypeStruct((2 * PART_ROWS, LANE), bf16)],
        where,
        hidden,
        other_hidden,
        gate_weight[0],
        up_weight[0],
        other_rows,
        scalars=1,
    )
    own_share, far_share = call(
        merge_kernel,
        [jax.ShapeDtypeStruct((PART_ROWS, LANE), f32), jax.ShapeDtypeStruct((PART_ROWS, LANE), bf16)],
        kept,
        swap(sent, across, 0),
    )
    summed = call(
        sum_kernel,
        [jax.ShapeDtypeStruct((HOME_ROWS, LANE), bf16)] * GROUP,
        own_share,
        swap(far_share, across, 1),
    )
    home = [summed[0]] + [from_behind(summed[o], "node", -o) for o in range(1, GROUP)]
    input_grad, gate_grad = call(
        unpack_kernel,
        [jax.ShapeDtypeStruct((FEAT, TOK), bf16), jax.ShapeDtypeStruct((2, TOK), f32)],
        route,
        gate_fixed.T,
        *home,
    )
    return input_grad.T, gate_grad.T


def solution(mesh):
    in_specs = (
        P("node", "local"),
        P("node", "local"),
        P("node", None, "local"),
        P("node", None, "local"),
        P("node", "local", None),
        P("node", None),
        P("node", None),
    )
    out_specs = (P("node", "local"), P("node", None))
    return jax.shard_map(body, mesh=mesh, in_specs=in_specs, out_specs=out_specs, check_vma=False)
```

```python
import jax
import jax.numpy as jnp
from jax import lax
from jax.experimental import pallas as pl
from jax.experimental.pallas import tpu as pltpu
from jax.sharding import PartitionSpec as P

GROUP = 4
CAP = 80
TOK = 128
LANE = 128
FEAT = 448
HID = 128
LOCAL = 8
ROUTED = GROUP * CAP
OUT_ROWS = 7 * CAP + 16
SHARD_ROWS = GROUP * 7 * CAP + 16
PART_ROWS = 3 * ROUTED + 2 * CAP + 16
HOME_ROWS = 4 * CAP + 16
HIDE_ROWS = 2 * ROUTED + 16
SHARES = LOCAL // 2
HALF_ROWS = SHARES * FEAT
LEVELS = 15
INTERPRET = False
LIMIT = 10

f32 = jnp.float32
bf16 = jnp.bfloat16
NT = (((1,), (1,)), ((), ()))
TN = (((0,), (0,)), ((), ()))


def from_behind(value, axis, steps):
    count = lax.axis_size(axis)
    pairs = [(source, (source + steps) % count) for source in range(count)]
    return lax.ppermute(value, axis, pairs)


def beside(core, place):
    return (place + 1 - 2 * ((place + core) & 1)) & 7


def across(core, place):
    return ((((place - 2 * core) & 7) ^ 2) + 2 * core) & 7


def swap(value, partner, turn):
    nodes, count = lax.axis_size("node"), lax.axis_size("local")
    pairs = [
        (node * count + place, node * count + partner((node + turn) & 1, place))
        for node in range(nodes)
        for place in range(count)
    ]
    return lax.ppermute(value, ("node", "local"), pairs)


def targets(core, place):
    return place, across(1 - core, place), across(core, place), (place + 4) & 7


def pick_kernel(where_ref, gate_ref, up_ref, out_ref, sems):
    core = where_ref[0] & 1
    theirs = targets(core, beside(core, where_ref[1]))
    copies = []
    for turn in range(SHARES):
        start = pl.multiple_of(theirs[turn] * FEAT, 64)
        for half, ref in enumerate((gate_ref, up_ref)):
            low = half * HALF_ROWS + turn * FEAT
            copies.append(
                pltpu.make_async_copy(
                    ref.at[pl.ds(start, FEAT), :], out_ref.at[low : low + FEAT, :], sems.at[2 * turn + half]
                )
            )
    for copy in copies:
        copy.start()
    for copy in copies:
        copy.wait()


def tables(route):
    offsets = lax.broadcasted_iota(jnp.int32, (8, TOK), 0)
    first = jnp.broadcast_to(route[0:1], (8, TOK)) == offsets
    second = jnp.broadcast_to(route[1:2], (8, TOK)) == offsets
    chosen = jnp.where(first | second, 1.0, 0.0)
    before = lax.broadcasted_iota(jnp.int32, (TOK, TOK), 0) < lax.broadcasted_iota(jnp.int32, (TOK, TOK), 1)
    ranks = jnp.dot(chosen.astype(bf16), jnp.where(before, 1.0, 0.0).astype(bf16), preferred_element_type=f32)
    ranks = jnp.where(chosen > 0.5, ranks, -1.0)
    slots = lax.broadcasted_iota(jnp.int32, (CAP, TOK), 0).astype(f32)
    return [
        jnp.where(slots == jnp.broadcast_to(ranks[o : o + 1], (CAP, TOK)), 1.0, 0.0).astype(bf16)
        for o in range(GROUP)
    ]


def level_of(top):
    level = jnp.zeros_like(top)
    for step in range(1, LEVELS):
        level = level + jnp.where(top < 2.0 ** (3 - 8 * step), 1.0, 0.0)
    return level


def power_of(level, sign):
    power = jnp.full_like(level, 2.0 ** (sign * 12))
    for step in range(1, LEVELS):
        power = jnp.where(level > step - 0.5, 2.0 ** (sign * (12 + 8 * step)), power)
    return power


def scaled(values):
    wide = values.astype(f32)
    top = jnp.max(jnp.max(jnp.abs(wide), axis=0, keepdims=True), axis=1, keepdims=True)
    level = level_of(jnp.broadcast_to(top, (1, TOK)))
    return (wide * power_of(level, 1)).astype(bf16), level


def pack_kernel(route_hbm, in_hbm, grad_hbm, *refs):
    out_refs = refs[0:GROUP]
    route_ref, in_ref, grad_ref, sems = refs[GROUP:]
    copies = [
        pltpu.make_async_copy(source, target, sems.at[number])
        for number, (source, target) in enumerate(((route_hbm, route_ref), (in_hbm, in_ref), (grad_hbm, grad_ref)))
    ]
    for copy in copies:
        copy.start()
    for copy in copies:
        copy.wait()
    table = jnp.concatenate(tables(route_ref[...]), axis=0)
    rows_in, level_in = scaled(in_ref[...])
    rows_grad, level_grad = scaled(grad_ref[...])
    tail = jnp.concatenate([rows_in[384:448], rows_grad[384:448]], axis=0)
    parts = [rows_in[0:128], rows_in[128:256], rows_in[256:384]]
    parts += [rows_grad[0:128], rows_grad[128:256], rows_grad[256:384], tail]
    for place, part in enumerate(parts):
        packed = lax.dot_general(table, part, NT, preferred_element_type=f32).astype(bf16)
        for o in range(GROUP):
            out_refs[o][place * CAP : (place + 1) * CAP, :] = packed[o * CAP : (o + 1) * CAP]
    line = lax.broadcasted_iota(jnp.int32, (16, LANE), 0)
    for o in range(GROUP):
        levels = jnp.where(line == 2 * o, level_in, jnp.where(line == 2 * o + 1, level_grad, 0.0))
        out_refs[o][7 * CAP : OUT_ROWS, :] = levels.astype(bf16)


def join_kernel(*all_refs):
    refs, out_ref = all_refs[0:GROUP][::-1], all_refs[GROUP]
    levels = jnp.zeros((16, LANE), bf16)
    for o in range(GROUP):
        out_ref[o * 7 * CAP : (o + 1) * 7 * CAP, :] = refs[o][0 : 7 * CAP, :]
        levels = levels + refs[o][7 * CAP : OUT_ROWS, :]
    out_ref[GROUP * 7 * CAP : SHARD_ROWS, :] = levels


def hidden_kernel(got_ref, gate_ref, up_ref, down_ref, out_ref):
    zero_cols = jnp.zeros((64, 2 * HID), bf16)
    zero_half = jnp.zeros((64, HID), bf16)
    pre = jnp.zeros((ROUTED, 2 * HID), f32)
    grad = jnp.zeros((ROUTED, HID), f32)

    def rows_of(d, o, place):
        start = d * SHARD_ROWS + (o * 7 + place) * CAP
        return got_ref[start : start + CAP, :]

    def column(d, place):
        return jnp.concatenate([rows_of(d, o, place) for o in range(GROUP)], axis=0)

    for d in range(LOCAL):
        low = d * FEAT
        tail = column(d, 6)
        in_a = jnp.concatenate([column(d, 0), column(d, 1)], axis=1)
        in_b = jnp.concatenate([column(d, 2), tail], axis=1)
        grad_a = jnp.concatenate([column(d, 3), column(d, 4)], axis=1)
        grad_b = jnp.concatenate([column(d, 5), tail], axis=1)
        both = jnp.concatenate([gate_ref[low : low + FEAT, :], up_ref[low : low + FEAT, :]], axis=1)
        down = down_ref[low : low + FEAT, :]
        both_b = jnp.concatenate([both[256:448], zero_cols], axis=0)
        down_b = jnp.concatenate([down[256:384], zero_half, down[384:448]], axis=0)
        part = jnp.dot(in_a, both[0:256], preferred_element_type=f32)
        part = part + jnp.dot(in_b, both_b, preferred_element_type=f32)
        part_grad = jnp.dot(grad_a, down[0:256], preferred_element_type=f32)
        part_grad = part_grad + jnp.dot(grad_b, down_b, preferred_element_type=f32)
        back_in = []
        back_grad = []
        levels = got_ref[(d + 1) * SHARD_ROWS - 16 : (d + 1) * SHARD_ROWS, :].astype(f32)
        for o in range(GROUP):
            inverse_in = power_of(levels[2 * o : 2 * o + 1], -1)
            inverse_grad = power_of(levels[2 * o + 1 : 2 * o + 2], -1)
            back_in.append(part[o * CAP : (o + 1) * CAP] * jnp.concatenate([inverse_in, inverse_in], axis=1))
            back_grad.append(part_grad[o * CAP : (o + 1) * CAP] * inverse_grad)
        pre = pre + jnp.concatenate(back_in, axis=0)
        grad = grad + jnp.concatenate(back_grad, axis=0)
    gate_pre = pre[:, 0:HID]
    up_pre = pre[:, HID : 2 * HID]
    sigmoid = jax.nn.sigmoid(gate_pre)
    swish = gate_pre * sigmoid
    product = swish * up_pre * grad
    up_grad = (grad * swish).astype(bf16)
    pre_grad = (grad * up_pre * sigmoid * (1.0 + gate_pre * (1.0 - sigmoid))).astype(bf16)
    line = lax.broadcasted_iota(jnp.int32, (16, LANE), 0)
    gate_rows = jnp.zeros((16, LANE), f32)
    for o in range(GROUP):
        piece = jnp.concatenate([product[o * CAP : (o + 1) * CAP], jnp.zeros((LANE - CAP, HID), f32)], axis=0)
        total = lax.dot_general(
            jnp.ones((8, HID), f32), piece, NT, preferred_element_type=f32, precision=lax.Precision.HIGHEST
        )[0:1]
        gate_rows = with_gate(gate_rows, line, o, total)
    out_ref[0:ROUTED, :] = pre_grad
    out_ref[ROUTED : 2 * ROUTED, :] = up_grad
    out_ref[2 * ROUTED : HIDE_ROWS, :] = gate_rows.astype(bf16)


def with_gate(rows, line, o, total):
    high = total.astype(bf16).astype(f32)
    return jnp.where(line == 2 * o, high, jnp.where(line == 2 * o + 1, total - high, rows))


def back_kernel(where_ref, own_ref, other_ref, own_gate_ref, own_up_ref, other_ref_rows, kept_ref, sent_ref):
    mine = targets(where_ref[0] & 1, where_ref[1])
    zero_cols = jnp.zeros((64, 4 * HID), bf16)
    hidden = jnp.concatenate(
        [
            own_ref[0:ROUTED, :],
            own_ref[ROUTED : 2 * ROUTED, :],
            other_ref[0:ROUTED, :],
            other_ref[ROUTED : 2 * ROUTED, :],
        ],
        axis=1,
    )
    paired = jnp.concatenate([hidden[0 : 2 * CAP], hidden[2 * CAP : 4 * CAP]], axis=1)
    own_gates = own_ref[2 * ROUTED : HIDE_ROWS, :].astype(f32)
    other_gates = other_ref[2 * ROUTED : HIDE_ROWS, :].astype(f32)
    line = lax.broadcasted_iota(jnp.int32, (16, LANE), 0)
    gate_rows = jnp.zeros((16, LANE), f32)
    for o in range(GROUP):
        own = own_gates[2 * o : 2 * o + 1] + own_gates[2 * o + 1 : 2 * o + 2]
        other = other_gates[2 * o : 2 * o + 1] + other_gates[2 * o + 1 : 2 * o + 2]
        gate_rows = with_gate(gate_rows, line, o, own + other)
    for d in range(SHARES):
        low = d * FEAT
        base = d % 2 * PART_ROWS
        out_ref = kept_ref if d < 2 else sent_ref
        kind = f32 if d < 2 else bf16
        start = pl.multiple_of(mine[d] * FEAT, 64)
        weights = jnp.concatenate(
            [
                own_gate_ref[pl.ds(start, FEAT), :],
                own_up_ref[pl.ds(start, FEAT), :],
                other_ref_rows[low : low + FEAT, :],
                other_ref_rows[HALF_ROWS + low : HALF_ROWS + low + FEAT, :],
            ],
            axis=1,
        )
        wide = lax.dot_general(hidden, weights[0:384], NT, preferred_element_type=f32).astype(kind)
        for j in range(3):
            out_ref[base + j * ROUTED : base + (j + 1) * ROUTED, :] = wide[:, j * LANE : (j + 1) * LANE]
        corner = jnp.concatenate([weights[384:448], zero_cols], axis=1)
        other = jnp.concatenate([zero_cols, weights[384:448]], axis=1)
        ends = jnp.concatenate([corner, other], axis=0)
        tail = lax.dot_general(paired, ends, NT, preferred_element_type=f32).astype(kind)
        out_ref[base + 3 * ROUTED : base + 3 * ROUTED + 2 * CAP, :] = tail
        out_ref[base + 3 * ROUTED + 2 * CAP : base + PART_ROWS, :] = gate_rows.astype(kind)


def merge_kernel(kept_ref, got_ref, own_ref, sent_ref):
    last = PART_ROWS - 16
    own_ref[...] = kept_ref[0:PART_ROWS, :] + got_ref[0:PART_ROWS, :].astype(f32)
    sent_ref[0:last, :] = (
        kept_ref[PART_ROWS : PART_ROWS + last, :] + got_ref[PART_ROWS : PART_ROWS + last, :].astype(f32)
    ).astype(bf16)
    gates = kept_ref[PART_ROWS + last :, :] + got_ref[PART_ROWS + last :, :].astype(f32)
    line = lax.broadcasted_iota(jnp.int32, (16, LANE), 0)
    rows = jnp.zeros((16, LANE), f32)
    for o in range(GROUP):
        rows = with_gate(rows, line, o, gates[2 * o : 2 * o + 1] + gates[2 * o + 1 : 2 * o + 2])
    sent_ref[last:PART_ROWS, :] = rows.astype(bf16)


def sum_kernel(own_ref, got_ref, *out_refs):
    def total(start, rows):
        return own_ref[start : start + rows, :] + got_ref[start : start + rows, :].astype(f32)

    for j in range(3):
        for o in range(GROUP):
            out_refs[o][j * CAP : (j + 1) * CAP, :] = total(j * ROUTED + o * CAP, CAP).astype(bf16)
    for half in range(2):
        tail = total(3 * ROUTED + half * CAP, CAP).astype(bf16)
        out_refs[half][3 * CAP : 4 * CAP, :] = tail
        out_refs[half + 2][3 * CAP : 4 * CAP, :] = tail
    gates = total(3 * ROUTED + 2 * CAP, 16)
    line = lax.broadcasted_iota(jnp.int32, (16, LANE), 0)
    for o in range(GROUP):
        gate = gates[2 * o : 2 * o + 1] + gates[2 * o + 1 : 2 * o + 2]
        high = gate.astype(bf16).astype(f32)
        rows = jnp.where(line == 0, high, jnp.where(line == 1, gate - high, 0.0))
        out_refs[o][4 * CAP : HOME_ROWS, :] = rows.astype(bf16)


def unpack_kernel(route_ref, fixed_ref, *refs):
    got_refs = refs[0:GROUP][::-1]
    out_ref, gate_ref = refs[GROUP], refs[GROUP + 1]
    route = route_ref[...]
    weights = fixed_ref[...].astype(f32) / 65536.0
    table = tables(route)
    head = jnp.zeros((384, TOK), f32)
    tail = jnp.zeros((64, TOK), f32)
    gate = jnp.zeros((2, TOK), f32)
    for o in range(GROUP):
        got = got_refs[o]
        hits = route == o
        weight = jnp.sum(jnp.where(hits, weights, 0.0), axis=0, keepdims=True)
        rows = jnp.concatenate([got[j * CAP : (j + 1) * CAP, :] for j in range(4)], axis=1)
        back = lax.dot_general(rows, table[o], TN, preferred_element_type=f32)
        head = head + weight * back[0:384]
        tail = tail + weight * (back[384:448] if o < 2 else back[448:512])
        gates = jnp.dot(got[4 * CAP : HOME_ROWS, 0:CAP], table[o], preferred_element_type=f32)
        gate = gate + jnp.where(hits, gates[0:1] + gates[1:2], 0.0)
    out_ref[0:384, :] = head.astype(bf16)
    out_ref[384:448, :] = tail.astype(bf16)
    gate_ref[...] = gate


def call(kernel, outs, *args, scalars=0, far=0, scratch=()):
    spaces = [pltpu.SMEM] * scalars + [pltpu.HBM] * far
    spaces += [pltpu.VMEM] * (len(args) - len(spaces))
    many = isinstance(outs, list)
    if not INTERPRET:
        args = [a if s is pltpu.SMEM else pltpu.with_memory_space_constraint(a, s) for a, s in zip(args, spaces)]
    return pl.pallas_call(
        kernel,
        out_shape=outs,
        in_specs=[pl.BlockSpec(memory_space=space) for space in spaces],
        out_specs=[pl.BlockSpec(memory_space=pltpu.VMEM)] * len(outs) if many else pl.BlockSpec(memory_space=pltpu.VMEM),
        scratch_shapes=list(scratch),
        interpret=INTERPRET,
        compiler_params=pltpu.CompilerParams(vmem_limit_bytes=LIMIT * 1024 * 1024),
    )(*args)


def body(layer_input, output_grad, gate_weight, up_weight, down_weight, route_offset, gate_fixed):
    route = route_offset.T
    where = jnp.stack([lax.axis_index("node"), lax.axis_index("local")])
    picked = call(
        pick_kernel,
        jax.ShapeDtypeStruct((2 * HALF_ROWS, HID), bf16),
        where,
        gate_weight[0],
        up_weight[0],
        scalars=1,
        far=2,
        scratch=[pltpu.SemaphoreType.DMA((2 * SHARES,))],
    )
    other_rows = swap(picked, beside, 0)
    packed = call(
        pack_kernel,
        [jax.ShapeDtypeStruct((OUT_ROWS, LANE), bf16)] * GROUP,
        route,
        layer_input.T,
        output_grad.T,
        far=3,
        scratch=[
            pltpu.VMEM((2, TOK), jnp.int32),
            pltpu.VMEM((FEAT, TOK), bf16),
            pltpu.VMEM((FEAT, TOK), bf16),
            pltpu.SemaphoreType.DMA((3,)),
        ],
    )
    got = [packed[0]] + [from_behind(packed[o], "node", o) for o in range(GROUP - 1, 0, -1)][::-1]
    *got, down_cols = lax.optimization_barrier((*got[::-1], down_weight[0].T))
    got = got[::-1]
    shard = call(join_kernel, jax.ShapeDtypeStruct((SHARD_ROWS, LANE), bf16), *got[::-1]).astype(jnp.float16)
    full = lax.all_gather(shard, "local", axis=0, tiled=True).astype(bf16)
    hidden = call(
        hidden_kernel,
        jax.ShapeDtypeStruct((HIDE_ROWS, LANE), bf16),
        full,
        gate_weight[0],
        up_weight[0],
        down_cols,
    )
    other_hidden = swap(hidden, beside, 0)
    kept, sent = call(
        back_kernel,
        [jax.ShapeDtypeStruct((2 * PART_ROWS, LANE), f32), jax.ShapeDtypeStruct((2 * PART_ROWS, LANE), bf16)],
        where,
        hidden,
        other_hidden,
        gate_weight[0],
        up_weight[0],
        other_rows,
        scalars=1,
    )
    own_share, far_share = call(
        merge_kernel,
        [jax.ShapeDtypeStruct((PART_ROWS, LANE), f32), jax.ShapeDtypeStruct((PART_ROWS, LANE), bf16)],
        kept,
        swap(sent, across, 0),
    )
    summed = call(
        sum_kernel,
        [jax.ShapeDtypeStruct((HOME_ROWS, LANE), bf16)] * GROUP,
        own_share,
        swap(far_share, across, 1),
    )
    home = [summed[0]] + [from_behind(summed[o], "node", -o) for o in range(GROUP - 1, 0, -1)][::-1]
    input_grad, gate_grad = call(
        unpack_kernel,
        [jax.ShapeDtypeStruct((FEAT, TOK), bf16), jax.ShapeDtypeStruct((2, TOK), f32)],
        route,
        gate_fixed.T,
        *home[::-1],
    )
    return input_grad.T, gate_grad.T


def solution(mesh):
    in_specs = (
        P("node", "local"),
        P("node", "local"),
        P("node", None, "local"),
        P("node", None, "local"),
        P("node", "local", None),
        P("node", None),
        P("node", None),
    )
    out_specs = (P("node", "local"), P("node", None))
    return jax.shard_map(body, mesh=mesh, in_specs=in_specs, out_specs=out_specs, check_vma=False)
```
